32 devices in a mesh: dp: 2 (over x), layer: 4 (over y, core), tensor: 4 (over z).
Axes of the slice: x: 2, y: 2, z: 4, core: 2. Of those that a mesh axis runs over, the one named last changes fastest.
Arguments:
- embeddings: bfloat16 [256, 4096], P('dp', 'tensor'), may hold values from -180 to 180
- layer_weight: bfloat16 [8, 4096, 4096], P('layer', None, 'tensor'), may hold values from -0.09375 to 0.09375
- rotation: float32 [4096, 4096], P(('dp', 'layer'), 'tensor'), may hold values from -3.2 to 3.2
Outputs:
- updated_rotation: float32 [4096, 4096], P(('dp', 'layer'), 'tensor')
The draws below stay inside these ranges and needn't reach their ends.
All inputs are finite; a program needn't handle non-finite values.
Results may differ from the reference program's by a relative error of at most 0.0042.
Values may be sent and summed in bfloat16 or wider, within the bound.
A program may use at most 128 MiB of HBM per device.

```python
import math
import jax
import jax.numpy as jnp
from jax import lax

D = 4096
TOKENS = 256
LAYERS = 8


def draw_embeddings(key, part):
    first_key, second_key = jax.random.split(key, 2)
    column = jnp.arange(D, dtype=jnp.float32) / D
    base = jnp.clip(jax.random.normal(first_key, (TOKENS, D), jnp.float32), -6.0, 6.0)
    trend = jnp.exp(math.log(10.0) * column)
    jitter = jnp.exp(jax.random.uniform(second_key, (D,), jnp.float32, 0.0, math.log(3.0)))
    return (base * (trend * jitter)[None, :]).astype(jnp.bfloat16)


def sign_parity(index):
    total = jnp.zeros((D, D), jnp.int32)
    for level in range(D.bit_length() - 1):
        row_bit = jnp.bitwise_and(jnp.right_shift(index, level), 1)
        total = total + row_bit[:, None] * row_bit[None, :]
    return total % 2


def draw_rotation(key, part):
    row_key, col_key, noise_key = jax.random.split(key, 3)
    index = jnp.arange(D, dtype=jnp.int32)
    parity = sign_parity(index)
    hadamard = (1 - 2 * parity).astype(jnp.float32)
    row_sign = (2 * jax.random.randint(row_key, (D,), 0, 2) - 1).astype(jnp.float32)
    col_sign = (2 * jax.random.randint(col_key, (D,), 0, 2) - 1).astype(jnp.float32)
    noise = 0.6 * jnp.clip(jax.random.normal(noise_key, (D, D), jnp.float32), -4.0, 4.0)
    return 0.8 * hadamard * row_sign[:, None] * col_sign[None, :] + noise


def levels(own_key, shape, cuts, least, high):
    def one(dim, shards_of):
        steps = jax.random.uniform(jax.random.fold_in(jax.random.fold_in(own_key, 6), dim), (shards_of,), jnp.float32, least / len(cuts), high / len(cuts))
        return jnp.repeat(jnp.exp(steps), shape[dim] // shards_of).reshape((-1,) + (1,) * (len(shape) - dim - 1))

    factor_of = one(*cuts[0])
    for cut in cuts[1:]:
        factor_of = factor_of * one(*cut)
    return factor_of


def scatter_about(stream_key, shape, deviation, reach, shards=(), kind=jnp.bfloat16):
    result = deviation * jax.random.normal(stream_key, shape, jnp.float32)
    if shards:
        result = result * levels(stream_key, shape, shards, -0.22, 0.18)
    return jnp.clip(result, -reach, reach).astype(kind)


def setup_inputs(seed: int = 0) -> dict:
    keys = jax.random.split(jax.random.key(seed), 4)
    embeddings = draw_embeddings(jax.random.fold_in(keys[3], 71), 0)
    layer_weight = scatter_about(keys[1], (LAYERS, D, D), D ** -0.5, 0.09375, ((0, 4), (2, 4)))
    rotation = draw_rotation(jax.random.fold_in(keys[3], 71), 0)
    return {"embeddings": embeddings, "layer_weight": layer_weight, "rotation": rotation}


def reference(embeddings, layer_weight, rotation):
    exact_mode = lax.Precision.HIGHEST
    root_width = math.sqrt(D)
    rotated = rotation / root_width
    hidden = embeddings
    gradient = jnp.zeros((D, D), jnp.float32)
    for level in range(LAYERS):
        widened = hidden.astype(jnp.float32)
        inverse = lax.rsqrt(lax.optimization_barrier(jnp.mean(widened * widened, axis=-1, keepdims=True)) + 1e-05)
        normed = (widened * inverse).astype(jnp.bfloat16)
        normed_wide = normed.astype(jnp.float32)
        projected = jnp.dot(normed_wide, rotated, precision=exact_mode)
        cubed = projected * projected * projected
        gradient = gradient + jnp.dot(normed_wide.T, cubed, precision=exact_mode)
        update = jnp.dot(normed, layer_weight[level], preferred_element_type=jnp.float32)
        hidden = (widened + update).astype(jnp.bfloat16)
    gradient = gradient / TOKENS
    cross = jnp.dot(gradient, rotated.T, precision=exact_mode)
    skew = cross - cross.T
    mean_square = jnp.mean(skew * skew)
    step_size = 0.5 / jnp.sqrt(D * (mean_square + 1e-06))
    first_product = jnp.dot(skew, rotated, precision=exact_mode)
    first_guess = rotated - step_size * first_product
    second_product = jnp.dot(skew, first_guess, precision=exact_mode)
    refined = rotated - 0.5 * step_size * (first_product + second_product)
    return root_width * refined
```

```python
import functools
import math

import jax
import jax.numpy as jnp
from jax import lax
from jax.experimental import pallas as pl
from jax.experimental.pallas import tpu as pltpu
from jax.sharding import PartitionSpec as P

ROWS = ("dp", "layer")
EVERY = ("dp", "layer", "tensor")
HALF = jnp.bfloat16
CHUNKS = 2
MESH = pl.DeviceIdType.MESH


def product(left, right, left_dim=1, right_dim=0):
    dims = (((left_dim,), (right_dim,)), ((), ()))
    return lax.dot_general(left, right, dims, preferred_element_type=jnp.float32)


def layers_kernel(chunks, embeddings, weight_hbm, records, hidden, outbox, weight, send_sem, recv_sem, weight_sem):
    dp, section, me = (lax.axis_index(name) for name in EVERY)
    sections, columns = lax.axis_size("layer"), lax.axis_size("tensor")
    levels = weight_hbm.shape[0]
    width = embeddings.shape[1]
    rows = embeddings.shape[0] // chunks
    tile = min(256, width)

    loads = [
        pltpu.make_async_copy(weight_hbm.at[level], weight.at[level], weight_sem.at[level])
        for level in range(levels)
    ]
    for load in loads:
        load.start()

    barrier = pltpu.get_barrier_semaphore()

    def greet(row, column):
        pl.semaphore_signal(barrier, inc=1, device_id=(dp, row, column), device_id_type=MESH)

    for column in range(columns):
        pl.when(column != me)(lambda column=column: greet(section, column))
        pl.when(section > 0)(lambda column=column: greet(section - 1, column))
        pl.when(section + 1 < sections)(lambda column=column: greet(section + 1, column))
    edges = jnp.where(section > 0, 1, 0) + jnp.where(section + 1 < sections, 1, 0)
    pl.semaphore_wait(barrier, columns - 1 + columns * edges)

    def copy(stage, chunk, source, column):
        level, row = (stage, section) if stage < levels else (0, section + 1)
        return pltpu.make_async_remote_copy(
            src_ref=source,
            dst_ref=hidden.at[level, chunk, me],
            send_sem=send_sem.at[stage, chunk, column],
            recv_sem=recv_sem.at[level, chunk, me],
            device_id=(dp, row, column),
            device_id_type=MESH,
        )

    def source_of(stage, chunk):
        return hidden.at[stage, chunk, me] if stage < levels else outbox.at[chunk]

    def sends(stage, chunk, action):
        for column in range(columns):
            if stage == 0:
                wanted = (section == 0) & (column != me)
            elif stage < levels:
                wanted = column != me
            else:
                wanted = section + 1 < sections
            pl.when(wanted)(lambda column=column: action(copy(stage, chunk, source_of(stage, chunk), column)))

    def arrivals(level, chunk):
        for column in range(columns):
            wanted = column != me
            if level == 0:
                wanted = wanted | (section > 0)

            @pl.when(wanted)
            def _():
                pltpu.make_async_remote_copy(
                    src_ref=hidden.at[level, chunk, column],
                    dst_ref=hidden.at[level, chunk, column],
                    send_sem=send_sem.at[level, chunk, column],
                    recv_sem=recv_sem.at[level, chunk, column],
                    device_id=(dp, section, column),
                    device_id_type=MESH,
                ).wait_recv()

    for chunk in range(chunks):

        @pl.when(section == 0)
        def _():
            hidden[0, chunk, me] = embeddings[chunk * rows : (chunk + 1) * rows, :]

        sends(0, chunk, lambda one: one.start())

    for level in range(levels):
        for chunk in range(chunks):
            arrivals(level, chunk)
            total = jnp.zeros((rows, 1), jnp.float32)
            for column in range(columns):
                widened = hidden[level, chunk, column].astype(jnp.float32)
                total = total + jnp.sum(widened * widened, axis=-1, keepdims=True)
            inverse = lax.rsqrt(total / (columns * width) + 1e-05)
            for column in range(columns):
                widened = hidden[level, chunk, column].astype(jnp.float32)
                records[level, chunk, :, column * width : (column + 1) * width] = (widened * inverse).astype(HALF)
            if chunk == 0:
                loads[level].wait()

            def multiply(part, _):
                place = pl.ds(pl.multiple_of(part * tile, tile), tile)
                update = jnp.dot(
                    records[level, chunk], weight[level, :, place], preferred_element_type=jnp.float32
                )
                fresh = (hidden[level, chunk, me, :, place].astype(jnp.float32) + update).astype(HALF)
                if level + 1 < levels:
                    hidden[level + 1, chunk, me, :, place] = fresh
                else:
                    outbox[chunk, :, place] = fresh
                return 0

            lax.fori_loop(0, width // tile, multiply, 0)
            sends(level + 1, chunk, lambda one: one.start())
    for stage in range(levels + 1):
        for chunk in range(chunks):
            sends(stage, chunk, lambda one: one.wait_send())


def run_layers(embeddings, layer_weight):
    levels, full, width = layer_weight.shape
    tokens = embeddings.shape[0]
    columns = lax.axis_size("tensor")
    rows = tokens // CHUNKS
    records = pl.pallas_call(
        functools.partial(layers_kernel, CHUNKS),
        out_shape=jax.ShapeDtypeStruct((levels, CHUNKS, rows, full), HALF),
        in_specs=[pl.BlockSpec(memory_space=pltpu.VMEM), pl.BlockSpec(memory_space=pl.ANY)],
        out_specs=pl.BlockSpec(memory_space=pltpu.VMEM),
        scratch_shapes=[
            pltpu.VMEM((levels, CHUNKS, columns, rows, width), HALF),
            pltpu.VMEM((CHUNKS, rows, width), HALF),
            pltpu.VMEM((levels, full, width), HALF),
            pltpu.SemaphoreType.DMA((levels + 1, CHUNKS, columns)),
            pltpu.SemaphoreType.DMA((levels, CHUNKS, columns)),
            pltpu.SemaphoreType.DMA((levels,)),
        ],
        compiler_params=pltpu.CompilerParams(
            collective_id=0, has_side_effects=True, vmem_limit_bytes=40 * 1024 * 1024
        ),
        cost_estimate=pl.CostEstimate(
            flops=2 * tokens * full * width * levels * 40,
            bytes_accessed=layer_weight.size * 2 * 20,
            transcendentals=0,
        ),
    )(embeddings, layer_weight)
    return records.reshape(levels * tokens, full)


def update_kernel(
    tokens,
    acts,
    panel,
    own,
    out,
    cubes,
    partial,
    from_left,
    from_right,
    weights,
    acts_columns,
    acts_rows,
    acts_turned,
    weights_columns,
    weights_rows,
    projected,
    products,
    total,
    skew,
    first,
    norms_line,
    norms_plane,
    line_send,
    line_recv,
    spread_send,
    spread_recv,
    plane_send,
    plane_pass,
    plane_recv,
    swap_send,
    swap_recv,
    skew_send,
    skew_recv,
    norm_send,
    norm_recv,
):
    dp, section, me = (lax.axis_index(name) for name in EVERY)
    groups, sections, columns = (lax.axis_size(name) for name in EVERY)
    rows, full = acts.shape
    block, width = own.shape
    members = groups * sections
    chips = members // 2
    halves = sections // 2
    core = section % 2
    chip = dp * halves + section // 2
    row = dp * sections + section
    tile = min(256, width)
    part_rows = 128
    parts = rows // part_rows
    per_column = width // block

    def place(index, size):
        return pl.ds(pl.multiple_of(index * size, size), size)

    def member_id(index):
        return (index // sections, index % sections, me)

    def on_chip(index, which):
        return (index // halves, (index % halves) * 2 + which, me)

    def remote(source, target, send, recv, device):
        return pltpu.make_async_remote_copy(
            src_ref=source, dst_ref=target, send_sem=send, recv_sem=recv, device_id=device, device_id_type=MESH
        )

    def landed(target, recv):
        remote(target, target, recv, recv, (dp, section, me)).wait_recv()

    barrier = pltpu.get_barrier_semaphore()
    for step in range(1, members):
        pl.semaphore_signal(barrier, inc=1, device_id=member_id((row + step) % members), device_id_type=MESH)
    for step in range(1, columns):
        pl.semaphore_signal(barrier, inc=1, device_id=(dp, section, (me + step) % columns), device_id_type=MESH)
    pl.semaphore_wait(barrier, members - 1 + columns - 1)

    def plane_copies(kind, view):
        own_view = view(row)
        copies = [
            remote(own_view, own_view, plane_send.at[kind, step], plane_recv.at[kind, row], on_chip((chip + step) % chips, core))
            for step in range(1, chips)
        ]
        copies.append(
            remote(own_view, own_view, plane_send.at[kind, 0], plane_recv.at[kind, row], on_chip(chip, 1 - core))
        )
        return copies

    def pass_copy(kind, view, step):
        source = 2 * ((chip + step) % chips) + core
        piece = view(source)
        return source, remote(
            piece, piece, plane_pass.at[kind, step], plane_recv.at[kind, source], on_chip(chip, 1 - core)
        )

    def plane_start(kind, view):
        for one in plane_copies(kind, view):
            one.start()

    def plane_forward(kind, view, step):
        source, one = pass_copy(kind, view, step)
        landed(view(source), plane_recv.at[kind, source])
        one.start()

    def plane_forward_all(kind, view):
        for step in range(1, chips):
            plane_forward(kind, view, step)

    def plane_finish(kind, view):
        for step in range(chips):
            source = 2 * ((chip + step) % chips) + 1 - core
            landed(view(source), plane_recv.at[kind, source])

    def plane_sent(kind, view):
        for one in plane_copies(kind, view):
            one.wait_send()
        for step in range(1, chips):
            pass_copy(kind, view, step)[1].wait_send()

    def tall(ref, size):
        return lambda index: ref.at[place(index, size)]

    def strip(part):
        return lambda index: weights_columns.at[:, place(index * parts + part, part_rows)]

    acts_kind, projected_kind, products_kind, first_kind, strip_kind = 0, 1, 2, 3, 4

    acts_columns[place(row, rows)] = acts[:, place(me, width)]
    plane_start(acts_kind, tall(acts_columns, rows))

    def acts_swap(step):
        target = (row + step) % members
        return remote(
            acts.at[:, place(target, block)],
            acts_rows.at[place(row, rows)],
            swap_send.at[0, step],
            swap_recv.at[0, row],
            member_id(target),
        )

    for step in range(1, members):
        acts_swap(step).start()
    acts_rows[place(row, rows)] = acts[:, place(row, block)]

    def project(index, _):
        where = place(index, tile)
        value = product(acts[...], panel[:, where])
        projected[place(row, rows), where] = value.astype(HALF)
        cubes[:, where] = (value * value * value * (1.0 / tokens)).astype(HALF)
        return 0

    lax.fori_loop(0, width // tile, project, 0)

    def weigh(index, _):
        where = place(index, tile)
        partial[where] = product(panel[where], cubes[...], 1, 1).astype(HALF)
        return 0

    lax.fori_loop(0, full // tile, weigh, 0)

    def piece(ref, column, part):
        return ref.at[place(column, width), place(part, part_rows)]

    def line_copy(part, column, right, source):
        target = from_left if right else from_right
        way = 0 if right else 1
        return remote(
            piece(source, column, part),
            piece(target, column, part),
            line_send.at[part, column, way],
            line_recv.at[part, column, way],
            (dp, section, me + 1 if right else me - 1),
        )

    def add_into(target, column, part):
        lanes = place(part, part_rows)

        def one(index, _):
            where = place(column * (width // tile) + index, tile)
            target[where, lanes] = (
                target[where, lanes].astype(jnp.float32) + partial[where, lanes].astype(jnp.float32)
            ).astype(HALF)
            return 0

        lax.fori_loop(0, width // tile, one, 0)

    def first_sends(part):
        for step in range(columns - 1):
            right, left = columns - 1 - step, step
            pl.when(me == 0)(lambda: line_copy(part, right, True, partial).start())
            pl.when(me == columns - 1)(lambda: line_copy(part, left, False, partial).start())

    def relay_right(part, step):
        column = columns - 1 - step

        @pl.when((me > 0) & (me < column))
        def _():
            landed(piece(from_left, column, part), line_recv.at[part, column, 0])
            add_into(from_left, column, part)
            line_copy(part, column, True, from_left).start()

    def relay_left(part, step):
        column = step

        @pl.when((me < columns - 1) & (me > column))
        def _():
            landed(piece(from_right, column, part), line_recv.at[part, column, 1])
            add_into(from_right, column, part)
            line_copy(part, column, False, from_right).start()

    def relay(part, step):
        pl.when(me < columns // 2)(lambda: relay_right(part, step))
        relay_left(part, step)
        pl.when(me >= columns // 2)(lambda: relay_right(part, step))

    def line_sent(part):
        for column in range(columns):
            pl.when(me < column)(lambda: line_copy(part, column, True, partial).wait_send())
            pl.when(me > column)(lambda: line_copy(part, column, False, partial).wait_send())

    def settle(part):
        lanes = place(part, part_rows)
        pl.when(me > 0)(lambda: landed(piece(from_left, me, part), line_recv.at[part, me, 0]))
        pl.when(me < columns - 1)(lambda: landed(piece(from_right, me, part), line_recv.at[part, me, 1]))
        left = jnp.where(me > 0, 1.0, 0.0)
        right = jnp.where(me < columns - 1, 1.0, 0.0)

        def one(index, _):
            where = place(me * (width // tile) + index, tile)
            value = partial[where, lanes].astype(jnp.float32)
            value = value + jnp.where(left > 0.5, from_left[where, lanes].astype(jnp.float32), 0.0)
            value = value + jnp.where(right > 0.5, from_right[where, lanes].astype(jnp.float32), 0.0)
            final = value.astype(HALF)
            weights[where, lanes] = final
            weights_columns[place(index, tile), place(row * parts + part, part_rows)] = final
            return 0

        lax.fori_loop(0, width // tile, one, 0)

    def spread_copy(part, column, right):
        view = piece(weights, column, part)
        return remote(
            view,
            view,
            spread_send.at[part, column, 0 if right else 1],
            spread_recv.at[part, column],
            (dp, section, me + 1 if right else me - 1),
        )

    def weights_swap(part, target):
        return remote(
            weights.at[place(target, block), place(part, part_rows)],
            weights_rows.at[:, place(row * parts + part, part_rows)],
            swap_send.at[1 + part, target],
            swap_recv.at[1 + part, row],
            member_id(target),
        )

    def hand_out(part, column):
        for index in range(per_column):
            target = column * per_column + index
            pl.when(target != row)(lambda: weights_swap(part, target).start())

            @pl.when(target == row)
            def _():
                weights_rows[:, place(row * parts + part, part_rows)] = weights[
                    place(row, block), place(part, part_rows)
                ]

    def offer(part):
        pl.when(me + 1 < columns)(lambda: spread_copy(part, me, True).start())
        pl.when(me > 0)(lambda: spread_copy(part, me, False).start())
        plane_start(strip_kind + part, strip(part))
        hand_out(part, me)

    def spread(part, step):
        @pl.when(me >= step)
        def _():
            landed(piece(weights, me - step, part), spread_recv.at[part, me - step])
            pl.when(me + 1 < columns)(lambda: spread_copy(part, me - step, True).start())
            hand_out(part, me - step)

        @pl.when(me + step < columns)
        def _():
            landed(piece(weights, me + step, part), spread_recv.at[part, me + step])
            pl.when(me > 0)(lambda: spread_copy(part, me + step, False).start())
            hand_out(part, me + step)

    def spread_sent(part):
        for column in range(columns):
            pl.when((column <= me) & (me + 1 < columns))(lambda: spread_copy(part, column, True).wait_send())
            pl.when((column >= me) & (me > 0))(lambda: spread_copy(part, column, False).wait_send())

    for part in range(parts):
        first_sends(part)
    for part in range(parts):
        for step in range(columns - 1):
            relay(part, step)
            if part > 0:
                spread(part - 1, step + 1)
        settle(part)
        offer(part)
        if part == 0:
            plane_forward_all(acts_kind, tall(acts_columns, rows))
    plane_start(projected_kind, tall(projected, rows))
    for step in range(columns - 1):
        spread(parts - 1, step + 1)
        if step == 0:
            for part in range(parts - 1):
                plane_forward_all(strip_kind + part, strip(part))
            for other in range(1, members):
                source = (row + other) % members
                landed(acts_rows.at[place(source, rows)], swap_recv.at[0, source])

            def turn(index, _):
                acts_turned[:, place(index, rows)] = acts_rows[place(index, rows)].T
                return 0

            lax.fori_loop(0, members, turn, 0)
    plane_forward_all(strip_kind + parts - 1, strip(parts - 1))

    total[...] = jnp.zeros_like(total)

    def apply(index, _):
        where = place(index, tile)
        total[...] += product(weights[where], panel[where], 0, 0)
        return 0

    lax.fori_loop(0, full // tile, apply, 0)
    products[place(row, rows)] = total[...].astype(HALF)
    plane_start(products_kind, tall(products, rows))

    plane_finish(acts_kind, tall(acts_columns, rows))
    for part in range(parts):
        for other in range(1, members):
            source = (row + other) % members
            landed(weights_rows.at[:, place(source * parts + part, part_rows)], swap_recv.at[1 + part, source])
        plane_finish(strip_kind + part, strip(part))

    def build(index, squares):
        where = place(index, tile)
        value = product(acts_turned[...], weights_columns[where], 1, 1) - product(
            weights_rows[...], acts_columns[:, where]
        )
        skew[me, :, where] = value.astype(HALF)
        return squares + jnp.sum(value * value)

    squares = lax.fori_loop(0, width // tile, build, jnp.float32(0.0))

    def skew_copy(column, right):
        view = skew.at[column]
        return remote(
            view,
            view,
            skew_send.at[column, 0 if right else 1],
            skew_recv.at[column],
            (dp, section, me + 1 if right else me - 1),
        )

    pl.when(me + 1 < columns)(lambda: skew_copy(me, True).start())
    pl.when(me > 0)(lambda: skew_copy(me, False).start())

    def skew_pass(step):
        @pl.when(me >= step)
        def _():
            landed(skew.at[me - step], skew_recv.at[me - step])
            pl.when(me + 1 < columns)(lambda: skew_copy(me - step, True).start())

        @pl.when(me + step < columns)
        def _():
            landed(skew.at[me + step], skew_recv.at[me + step])
            pl.when(me > 0)(lambda: skew_copy(me + step, False).start())

    def skew_sent():
        for column in range(columns):
            pl.when((column <= me) & (me + 1 < columns))(lambda: skew_copy(column, True).wait_send())
            pl.when((column >= me) & (me > 0))(lambda: skew_copy(column, False).wait_send())

    norms_line[me] = jnp.full(norms_line.shape[1:], squares, jnp.float32)

    def norm_line_copy(step):
        other = (me + step) % columns
        return remote(
            norms_line.at[me], norms_line.at[me], norm_send.at[0, step], norm_recv.at[0, me], (dp, section, other)
        )

    def norm_plane_copy(step):
        return remote(
            norms_plane.at[row],
            norms_plane.at[row],
            norm_send.at[1, step],
            norm_recv.at[1, row],
            member_id((row + step) % members),
        )

    for step in range(1, columns):
        norm_line_copy(step).start()

    plane_forward_all(projected_kind, tall(projected, rows))
    plane_forward_all(products_kind, tall(products, rows))
    for step in range(1, columns):
        other = (me + step) % columns
        landed(norms_line.at[other], norm_recv.at[0, other])
    norms_plane[row] = jnp.sum(norms_line[...], axis=0)
    for step in range(1, members):
        norm_plane_copy(step).start()
    plane_finish(projected_kind, tall(projected, rows))
    plane_finish(products_kind, tall(products, rows))

    def multiply(index, _):
        where = place(index, tile)
        value = product(acts_turned[...], products[:, where]) - product(weights_rows[...], projected[:, where])
        out[:, where] = value
        first[place(row, block), where] = value.astype(HALF)
        return 0

    lax.fori_loop(0, width // tile, multiply, 0)
    plane_start(first_kind, tall(first, block))
    for step in range(1, max(chips, columns)):
        if step < columns:
            skew_pass(step)
        if step < chips:
            plane_forward(first_kind, tall(first, block), step)
    for step in range(1, members):
        other = (row + step) % members
        landed(norms_plane.at[other], norm_recv.at[1, other])
    plane_finish(first_kind, tall(first, block))

    mean_square = jnp.sum(norms_plane[...], axis=0)[0:1, 0:1] / (full * full)
    scale = 0.5 * lax.rsqrt(full * (mean_square + 1e-06))
    root = math.sqrt(full)

    def finish(index, _):
        where = place(index, tile)
        value = jnp.zeros((block, tile), jnp.float32)
        for column in range(columns):
            value = value + product(skew[column], first[column * width : (column + 1) * width, where])
        out[:, where] = own[:, where] - (root * scale) * out[:, where] + (0.5 * root * scale * scale) * value
        return 0

    lax.fori_loop(0, width // tile, finish, 0)

    for part in range(parts):
        line_sent(part)
        spread_sent(part)
        plane_sent(strip_kind + part, strip(part))
        for target in range(members):
            pl.when(target != row)(lambda: weights_swap(part, target).wait_send())
    for step in range(1, members):
        acts_swap(step).wait_send()
        norm_plane_copy(step).wait_send()
    for step in range(1, columns):
        norm_line_copy(step).wait_send()
    skew_sent()
    plane_sent(acts_kind, tall(acts_columns, rows))
    plane_sent(projected_kind, tall(projected, rows))
    plane_sent(products_kind, tall(products, rows))
    plane_sent(first_kind, tall(first, block))


def run_update(acts, panel, rotation, tokens):
    rows, full = acts.shape
    block, width = rotation.shape
    columns = lax.axis_size("tensor")
    members = lax.axis_size("dp") * lax.axis_size("layer")
    chips = members // 2
    parts = rows // 128
    kinds = 4 + parts
    held = members * rows
    dma = pltpu.SemaphoreType.DMA
    return pl.pallas_call(
        functools.partial(update_kernel, tokens),
        out_shape=jax.ShapeDtypeStruct((block, width), jnp.float32),
        in_specs=[pl.BlockSpec(memory_space=pltpu.VMEM)] * 3,
        out_specs=pl.BlockSpec(memory_space=pltpu.VMEM),
        scratch_shapes=[
            pltpu.VMEM((rows, width), HALF),
            pltpu.VMEM((full, rows), HALF),
            pltpu.VMEM((full, rows), HALF),
            pltpu.VMEM((full, rows), HALF),
            pltpu.VMEM((full, rows), HALF),
            pltpu.VMEM((held, width), HALF),
            pltpu.VMEM((held, block), HALF),
            pltpu.VMEM((block, held), HALF),
            pltpu.VMEM((width, held), HALF),
            pltpu.VMEM((block, held), HALF),
            pltpu.VMEM((held, width), HALF),
            pltpu.VMEM((held, width), HALF),
            pltpu.VMEM((rows, width), jnp.float32),
            pltpu.VMEM((columns, block, width), HALF),
            pltpu.VMEM((full, width), HALF),
            pltpu.VMEM((columns, 8, 128), jnp.float32),
            pltpu.VMEM((members, 8, 128), jnp.float32),
            dma((parts, columns, 2)),
            dma((parts, columns, 2)),
            dma((parts, columns, 2)),
            dma((parts, columns)),
            dma((kinds, chips)),
            dma((kinds, chips)),
            dma((kinds, members)),
            dma((1 + parts, members)),
            dma((1 + parts, members)),
            dma((columns, 2)),
            dma((columns,)),
            dma((2, max(members, columns))),
            dma((2, max(members, columns))),
        ],
        compiler_params=pltpu.CompilerParams(
            collective_id=1, has_side_effects=True, vmem_limit_bytes=62 * 1024 * 1024
        ),
        cost_estimate=pl.CostEstimate(
            flops=2 * full * full * full // 4, bytes_accessed=full * width * 8, transcendentals=0
        ),
    )(acts, panel, rotation)


def shards(embeddings, layer_weight, rotation):
    full = layer_weight.shape[1]
    head = (rotation / math.sqrt(full)).astype(HALF)
    panel = lax.all_gather(head, ROWS, axis=0, tiled=True)
    acts = run_layers(embeddings, layer_weight)
    return run_update(acts, panel, rotation, embeddings.shape[0] * lax.axis_size("dp"))


def solution(mesh):
    return jax.shard_map(
        shards,
        mesh=mesh,
        in_specs=(P("dp", "tensor"), P("layer", None, "tensor"), P(("dp", "layer"), "tensor")),
        out_specs=P(("dp", "layer"), "tensor"),
        check_vma=False,
    )
```

```python
import functools
import math

import jax
import jax.numpy as jnp
from jax import lax
from jax.experimental import pallas as pl
from jax.experimental.pallas import tpu as pltpu
from jax.sharding import PartitionSpec as P

ROWS = ("dp", "layer")
EVERY = ("dp", "layer", "tensor")
HALF = jnp.bfloat16
CHUNKS = 4
LAG = 2
REACH = 2
MESH = pl.DeviceIdType.MESH


def product(left, right, left_dim=1, right_dim=0):
    dims = (((left_dim,), (right_dim,)), ((), ()))
    return lax.dot_general(left, right, dims, preferred_element_type=jnp.float32)


def layers_kernel(
    chunks,
    embeddings,
    weight_hbm,
    records,
    hidden,
    outbox,
    weight,
    update,
    squares,
    send_sem,
    pass_sem,
    recv_sem,
    weight_sem,
):
    dp, section, me = (lax.axis_index(name) for name in EVERY)
    sections, columns = lax.axis_size("layer"), lax.axis_size("tensor")
    levels = weight_hbm.shape[0]
    width = embeddings.shape[1]
    rows = embeddings.shape[0] // chunks
    full = columns * width
    distances = []
    for base in range(0, columns - 1, REACH):
        group = [d for d in range(base + 1, base + REACH + 1) if d < columns]
        distances += group[-1:] + group[:-1] if base + REACH + 1 < columns else group

    loads = [
        pltpu.make_async_copy(weight_hbm.at[level], weight.at[level], weight_sem.at[level])
        for level in range(levels)
    ]
    for load in loads:
        load.start()

    barrier = pltpu.get_barrier_semaphore()

    def greet(row, column):
        pl.semaphore_signal(barrier, inc=1, device_id=(dp, row, column), device_id_type=MESH)

    for column in range(columns):
        pl.when(column != me)(lambda column=column: greet(section, column))
        pl.when(section > 0)(lambda column=column: greet(section - 1, column))
        pl.when(section + 1 < sections)(lambda column=column: greet(section + 1, column))
    edges = jnp.where(section > 0, 1, 0) + jnp.where(section + 1 < sections, 1, 0)
    pl.semaphore_wait(barrier, columns - 1 + columns * edges)

    def remote(source, target, send, recv, row, column):
        return pltpu.make_async_remote_copy(
            src_ref=source,
            dst_ref=target,
            send_sem=send,
            recv_sem=recv,
            device_id=(dp, row, column),
            device_id_type=MESH,
        )

    def own_copy(stage, chunk, offset):
        level, row = (stage, section) if stage < levels else (0, section + 1)
        source = hidden.at[stage, chunk, me] if stage < levels else outbox.at[chunk]
        return remote(
            source,
            hidden.at[level, chunk, me],
            send_sem.at[stage, chunk, offset + REACH],
            recv_sem.at[level, chunk, me],
            row,
            me + offset,
        )

    def own_copies(stage, chunk, action):
        for reach in range(REACH, -1, -1):
            for offset in (reach, -reach) if reach else (0,):
                wanted = (me + offset >= 0) & (me + offset < columns)
                if stage == levels:
                    wanted = wanted & (section + 1 < sections)
                elif offset == 0:
                    continue
                elif stage == 0:
                    wanted = wanted & (section == 0)
                pl.when(wanted)(lambda offset=offset: action(own_copy(stage, chunk, offset)))

    def pass_copy(level, chunk, source, offset):
        view = hidden.at[level, chunk, source]
        return remote(
            view,
            view,
            pass_sem.at[level, chunk, source, abs(offset) - 1],
            recv_sem.at[level, chunk, source],
            section,
            me + offset,
        )

    def passes(level, chunk, distance, way, action):
        if distance % REACH or distance + 1 >= columns:
            return
        source = me - way * distance
        for reach in range(REACH, 0, -1):
            target = me + way * reach
            pl.when((target >= 0) & (target < columns))(
                lambda reach=reach: action(pass_copy(level, chunk, source, way * reach))
            )

    def arrive(level, chunk, source):
        view = hidden.at[level, chunk, source]
        remote(view, view, recv_sem.at[level, chunk, source], recv_sem.at[level, chunk, source], section, me).wait_recv()

    def gather_in(level, chunk, source, first=False):
        value = hidden[level, chunk, source]
        wide = value.astype(jnp.float32)
        square = jnp.sum(wide * wide, axis=-1, keepdims=True)
        part = product(value, weight[level, pl.ds(pl.multiple_of(source * width, width), width), :])
        squares[...] = square if first else squares[...] + square
        update[...] = part if first else update[...] + part

    def step(level, chunk):
        if level == 0:
            pl.when(section > 0)(lambda: arrive(level, chunk, me))
        gather_in(level, chunk, me, True)
        for distance in distances:
            for way in (1, -1):
                source = me - way * distance

                @pl.when((source >= 0) & (source < columns))
                def _():
                    arrive(level, chunk, source)
                    passes(level, chunk, distance, way, lambda one: one.start())
                    gather_in(level, chunk, source)

        inverse = lax.rsqrt(squares[...] / full + 1e-05)
        fresh = (hidden[level, chunk, me].astype(jnp.float32) + inverse * update[...]).astype(HALF)
        if level + 1 < levels:
            hidden[level + 1, chunk, me] = fresh
        else:
            outbox[chunk] = fresh
        own_copies(level + 1, chunk, lambda one: one.start())
        for column in range(columns):
            wide = hidden[level, chunk, column].astype(jnp.float32)
            records[level, chunk, :, column * width : (column + 1) * width] = (wide * inverse).astype(HALF)

    @pl.when(section == 0)
    def _():
        for chunk in range(chunks):
            hidden[0, chunk, me] = embeddings[chunk * rows : (chunk + 1) * rows, :]

    for chunk in range(chunks):
        own_copies(0, chunk, lambda one: one.start())

    def turn(index, _):
        for level in range(levels):
            chunk = index - level * LAG

            @pl.when((chunk >= 0) & (chunk < chunks))
            def _():
                pl.when(chunk == 0)(lambda: loads[level].wait())
                step(level, chunk)

        return 0

    lax.fori_loop(0, chunks + (levels - 1) * LAG, turn, 0)

    for chunk in range(chunks):
        for stage in range(levels + 1):
            own_copies(stage, chunk, lambda one: one.wait_send())
        for level in range(levels):
            for distance in distances:
                for way in (1, -1):
                    source = me - way * distance
                    pl.when((source >= 0) & (source < columns))(
                        lambda distance=distance, way=way: passes(
                            level, chunk, distance, way, lambda one: one.wait_send()
                        )
                    )


def run_layers(embeddings, layer_weight):
    levels, full, width = layer_weight.shape
    tokens = embeddings.shape[0]
    columns = lax.axis_size("tensor")
    rows = tokens // CHUNKS
    dma = pltpu.SemaphoreType.DMA
    records = pl.pallas_call(
        functools.partial(layers_kernel, CHUNKS),
        out_shape=jax.ShapeDtypeStruct((levels, CHUNKS, rows, full), HALF),
        in_specs=[pl.BlockSpec(memory_space=pltpu.VMEM), pl.BlockSpec(memory_space=pl.ANY)],
        out_specs=pl.BlockSpec(memory_space=pltpu.VMEM),
        scratch_shapes=[
            pltpu.VMEM((levels, CHUNKS, columns, rows, width), HALF),
            pltpu.VMEM((CHUNKS, rows, width), HALF),
            pltpu.VMEM((levels, full, width), HALF),
            pltpu.VMEM((rows, width), jnp.float32),
            pltpu.VMEM((rows, 1), jnp.float32),
            dma((levels + 1, CHUNKS, 2 * REACH + 1)),
            dma((levels, CHUNKS, columns, REACH)),
            dma((levels, CHUNKS, columns)),
            dma((levels,)),
        ],
        compiler_params=pltpu.CompilerParams(
            collective_id=0, has_side_effects=True, vmem_limit_bytes=40 * 1024 * 1024
        ),
        cost_estimate=pl.CostEstimate(
            flops=2 * tokens * full * width * levels * 40,
            bytes_accessed=layer_weight.size * 2 * 20,
            transcendentals=0,
        ),
    )(embeddings, layer_weight)
    return records.reshape(levels * tokens, full)


def update_kernel(
    tokens,
    acts,
    panel_hbm,
    own_hbm,
    out,
    panel,
    own,
    cubes,
    partial,
    from_left,
    from_right,
    weights,
    acts_columns,
    acts_rows,
    acts_turned,
    weights_columns,
    weights_rows,
    projected,
    products,
    total,
    skew,
    first,
    norms_line,
    norms_plane,
    line_send,
    line_recv,
    spread_send,
    spread_recv,
    plane_send,
    plane_pass,
    plane_cross,
    plane_recv,
    swap_send,
    swap_recv,
    skew_send,
    skew_recv,
    norm_send,
    norm_recv,
    load_sem,
):
    dp, section, me = (lax.axis_index(name) for name in EVERY)
    groups, sections, columns = (lax.axis_size(name) for name in EVERY)
    loads = [
        pltpu.make_async_copy(panel_hbm, panel, load_sem.at[0]),
        pltpu.make_async_copy(own_hbm, own, load_sem.at[1]),
    ]
    for load in loads:
        load.start()
    rows, full = acts.shape
    block, width = own_hbm.shape
    members = groups * sections
    halves = sections // 2
    core = section % 2
    side = section // 2
    row = dp * sections + section
    tile = min(256, width)
    parts = 2
    part_rows = rows // parts
    per_column = width // block

    def place(index, size):
        return pl.ds(pl.multiple_of(index * size, size), size)

    def member_id(index):
        return (index // sections, index % sections, me)

    def at(across, along, which):
        return (dp + across) % groups, ((side + along) % halves) * 2 + which

    def index_of(spot):
        return spot[0] * sections + spot[1]

    def remote(source, target, send, recv, device):
        return pltpu.make_async_remote_copy(
            src_ref=source, dst_ref=target, send_sem=send, recv_sem=recv, device_id=device, device_id_type=MESH
        )

    def landed(target, recv):
        remote(target, target, recv, recv, (dp, section, me)).wait_recv()

    barrier = pltpu.get_barrier_semaphore()
    for step in range(1, members):
        pl.semaphore_signal(barrier, inc=1, device_id=member_id((row + step) % members), device_id_type=MESH)
    for step in range(1, columns):
        pl.semaphore_signal(barrier, inc=1, device_id=(dp, section, (me + step) % columns), device_id_type=MESH)
    pl.semaphore_wait(barrier, members - 1 + columns - 1)

    def send_to(view, source, half, spot, send, kind):
        piece = view(source, half)
        return remote(piece, piece, send, plane_recv.at[kind, source, half], (spot[0], spot[1], me))

    def plane_copies(kind, view, which=(0, 1)):
        def across(half):
            return [
                send_to(view, row, half, at(x, 0, core), plane_send.at[kind, half, x], kind) for x in range(1, groups)
            ]

        def along(half):
            return [
                send_to(view, row, half, at(0, y, core), plane_send.at[kind, half, groups + y], kind)
                for y in range(1, halves)
            ]

        def other(half):
            return [send_to(view, row, half, at(0, 0, 1 - core), plane_send.at[kind, half, 0], kind)]

        return [
            along(half) + across(half) + other(half) if half else across(half) + along(half) + other(half)
            for half in which
        ]

    def pass_copies(kind, view, x, y, half):
        source = index_of(at(x, y, core))
        copies = []
        if half == 0 and y == 0:
            copies += [
                send_to(view, source, half, at(0, z, core), plane_cross.at[kind, half, x, z], kind)
                for z in range(1, halves)
            ]
        if half == 1 and x == 0:
            copies += [
                send_to(view, source, half, at(z, 0, core), plane_cross.at[kind, half, z, y], kind)
                for z in range(1, groups)
            ]
        copies.append(send_to(view, source, half, at(0, 0, 1 - core), plane_pass.at[kind, half, x * halves + y], kind))
        return source, copies

    def plane_start(kind, view, which=(0, 1)):
        copies = plane_copies(kind, view, which)
        most = max(len(one) for one in copies)
        for spot in range(most):
            for one in copies:
                if spot < len(one):
                    one[spot].start()

    near = [(x, 0) for x in range(1, groups)]
    beside = [(0, y) for y in range(1, halves)]
    beyond = [(x, y) for x in range(1, groups) for y in range(1, halves)]

    def plane_take(kind, view, spots, half):
        for x, y in spots:
            source, copies = pass_copies(kind, view, x, y, half)
            landed(view(source, half), plane_recv.at[kind, source, half])
            for one in copies:
                one.start()

    def plane_relay(kind, view):
        plane_take(kind, view, near, 0)
        plane_take(kind, view, beside, 1)

    def plane_rest(kind, view):
        plane_take(kind, view, near, 1)
        plane_take(kind, view, beside, 0)
        for half in range(2):
            plane_take(kind, view, beyond, half)

    def plane_finish(kind, view):
        for x in range(groups):
            for y in range(halves):
                source = index_of(at(x, y, 1 - core))
                for half in range(2):
                    landed(view(source, half), plane_recv.at[kind, source, half])

    def plane_sent(kind, view):
        for copies in plane_copies(kind, view):
            for one in copies:
                one.wait_send()
        for half in range(2):
            for x, y in near + beside + beyond:
                for one in pass_copies(kind, view, x, y, half)[1]:
                    one.wait_send()

    def tall(ref, size):
        return lambda index, half: ref.at[place(2 * index + half, size // 2)]

    def strip(index, half):
        return weights_columns.at[:, place(2 * index + half, part_rows)]

    acts_kind, projected_kind, products_kind, first_kind, strip_kind = 0, 1, 2, 3, 4

    acts_columns[place(row, rows)] = acts[:, place(me, width)]
    plane_start(acts_kind, tall(acts_columns, rows))

    def acts_swap(step):
        target = (row + step) % members
        return remote(
            acts.at[:, place(target, block)],
            acts_rows.at[place(row, rows)],
            swap_send.at[0, step],
            swap_recv.at[0, row],
            member_id(target),
        )

    acts_rows[place(row, rows)] = acts[:, place(row, block)]
    loads[0].wait()

    def project(index, _):
        where = place(index, tile)
        value = product(acts[...], panel[:, where])
        projected[place(row, rows), where] = value.astype(HALF)
        cubes[:, where] = (value * value * value * (1.0 / tokens)).astype(HALF)
        return 0

    lax.fori_loop(0, width // tile, project, 0)
    plane_relay(acts_kind, tall(acts_columns, rows))
    for step in range(1, members):
        acts_swap(step).start()

    def weigh(index, _):
        where = place(index, width)
        partial[where] = product(panel[where], cubes[...], 1, 1).astype(HALF)
        return 0

    lax.fori_loop(0, columns, weigh, 0)

    def piece(ref, column, part):
        return ref.at[place(column, width), place(part, part_rows)]

    def line_copy(part, column, right, source):
        target = from_left if right else from_right
        way = 0 if right else 1
        return remote(
            piece(source, column, part),
            piece(target, column, part),
            line_send.at[part, column, way],
            line_recv.at[part, column, way],
            (dp, section, me + 1 if right else me - 1),
        )

    def add_into(target, column, part):
        lanes = place(part, part_rows)

        def one(index, _):
            where = place(column * (width // tile) + index, tile)
            target[where, lanes] = (
                target[where, lanes].astype(jnp.float32) + partial[where, lanes].astype(jnp.float32)
            ).astype(HALF)
            return 0

        lax.fori_loop(0, width // tile, one, 0)

    def first_sends(part, steps):
        for step in steps:
            right, left = columns - 1 - step, step
            pl.when(me == 0)(lambda: line_copy(part, right, True, partial).start())
            pl.when(me == columns - 1)(lambda: line_copy(part, left, False, partial).start())

    def relay_right(part, step):
        column = columns - 1 - step

        @pl.when((me > 0) & (me < column))
        def _():
            landed(piece(from_left, column, part), line_recv.at[part, column, 0])
            add_into(from_left, column, part)
            line_copy(part, column, True, from_left).start()

    def relay_left(part, step):
        column = step

        @pl.when((me < columns - 1) & (me > column))
        def _():
            landed(piece(from_right, column, part), line_recv.at[part, column, 1])
            add_into(from_right, column, part)
            line_copy(part, column, False, from_right).start()

    def relay(part, step):
        pl.when(me < columns // 2)(lambda: relay_right(part, step))
        relay_left(part, step)
        pl.when(me >= columns // 2)(lambda: relay_right(part, step))

    def line_sent(part):
        for column in range(columns):
            pl.when(me < column)(lambda: line_copy(part, column, True, partial).wait_send())
            pl.when(me > column)(lambda: line_copy(part, column, False, partial).wait_send())

    def settle(part):
        lanes = place(part, part_rows)
        pl.when(me > 0)(lambda: landed(piece(from_left, me, part), line_recv.at[part, me, 0]))
        pl.when(me < columns - 1)(lambda: landed(piece(from_right, me, part), line_recv.at[part, me, 1]))
        left = jnp.where(me > 0, 1.0, 0.0)
        right = jnp.where(me < columns - 1, 1.0, 0.0)

        def one(index, _):
            where = place(me * (width // tile) + index, tile)
            value = partial[where, lanes].astype(jnp.float32)
            value = value + jnp.where(left > 0.5, from_left[where, lanes].astype(jnp.float32), 0.0)
            value = value + jnp.where(right > 0.5, from_right[where, lanes].astype(jnp.float32), 0.0)
            final = value.astype(HALF)
            weights[where, lanes] = final
            weights_columns[place(index, tile), place(row * parts + part, part_rows)] = final
            return 0

        lax.fori_loop(0, width // tile, one, 0)

    def spread_copy(part, column, right):
        view = piece(weights, column, part)
        return remote(
            view,
            view,
            spread_send.at[part, column, 0 if right else 1],
            spread_recv.at[part, column],
            (dp, section, me + 1 if right else me - 1),
        )

    def weights_swap(part, target):
        return remote(
            weights.at[place(target, block), place(part, part_rows)],
            weights_rows.at[:, place(row * parts + part, part_rows)],
            swap_send.at[1 + part, target],
            swap_recv.at[1 + part, row],
            member_id(target),
        )

    def hand_out(part, column):
        for index in range(per_column):
            target = column * per_column + index
            pl.when(target != row)(lambda: weights_swap(part, target).start())

            @pl.when(target == row)
            def _():
                weights_rows[:, place(row * parts + part, part_rows)] = weights[
                    place(row, block), place(part, part_rows)
                ]

    def offer(part):
        pl.when(me + 1 < columns)(lambda: spread_copy(part, me, True).start())
        pl.when(me > 0)(lambda: spread_copy(part, me, False).start())
        plane_start(strip_kind, strip, (part,))
        hand_out(part, me)

    def spread(part, step):
        @pl.when(me >= step)
        def _():
            landed(piece(weights, me - step, part), spread_recv.at[part, me - step])
            pl.when(me + 1 < columns)(lambda: spread_copy(part, me - step, True).start())
            hand_out(part, me - step)

        @pl.when(me + step < columns)
        def _():
            landed(piece(weights, me + step, part), spread_recv.at[part, me + step])
            pl.when(me > 0)(lambda: spread_copy(part, me + step, False).start())
            hand_out(part, me + step)

    def spread_sent(part):
        for column in range(columns):
            pl.when((column <= me) & (me + 1 < columns))(lambda: spread_copy(part, column, True).wait_send())
            pl.when((column >= me) & (me > 0))(lambda: spread_copy(part, column, False).wait_send())

    steps = range(columns - 1)
    first_sends(0, steps)
    first_sends(1, steps[:1])
    for step in steps:
        relay(0, step)
    settle(0)
    offer(0)
    first_sends(1, steps[1:])
    for step in steps:
        relay(1, step)
        spread(0, step + 1)
    settle(1)
    offer(1)
    plane_take(strip_kind, strip, near, 0)
    plane_rest(acts_kind, tall(acts_columns, rows))
    for other in range(1, members):
        source = (row + other) % members
        landed(acts_rows.at[place(source, rows)], swap_recv.at[0, source])

    def turn(index, _):
        acts_turned[:, place(index, rows)] = acts_rows[place(index, rows)].T
        return 0

    for step in steps:
        spread(1, step + 1)
        if step == 0:
            plane_take(strip_kind, strip, beside, 1)
    lax.fori_loop(0, members, turn, 0)

    def apply(index, _):
        where = place(index, width)
        total[...] += product(weights[where], panel[where], 0, 0)
        return 0

    total[...] = jnp.zeros_like(total)
    lax.fori_loop(0, columns, apply, 0)
    products[place(row, rows)] = total[...].astype(HALF)
    plane_start(products_kind, tall(products, rows))
    plane_start(projected_kind, tall(projected, rows))

    plane_rest(strip_kind, strip)
    plane_finish(acts_kind, tall(acts_columns, rows))
    for part in range(parts):
        for other in range(1, members):
            source = (row + other) % members
            landed(weights_rows.at[:, place(source * parts + part, part_rows)], swap_recv.at[1 + part, source])
    plane_finish(strip_kind, strip)

    def build(index, squares):
        where = place(index, tile)
        value = product(acts_turned[...], weights_columns[where], 1, 1) - product(
            weights_rows[...], acts_columns[:, where]
        )
        skew[me, :, where] = value.astype(HALF)
        return squares + jnp.sum(value * value)

    squares = lax.fori_loop(0, width // tile, build, jnp.float32(0.0))

    def skew_copy(column, right):
        view = skew.at[column]
        return remote(
            view,
            view,
            skew_send.at[column, 0 if right else 1],
            skew_recv.at[column],
            (dp, section, me + 1 if right else me - 1),
        )

    pl.when(me + 1 < columns)(lambda: skew_copy(me, True).start())
    pl.when(me > 0)(lambda: skew_copy(me, False).start())

    def skew_pass(step):
        @pl.when(me >= step)
        def _():
            landed(skew.at[me - step], skew_recv.at[me - step])
            pl.when(me + 1 < columns)(lambda: skew_copy(me - step, True).start())

        @pl.when(me + step < columns)
        def _():
            landed(skew.at[me + step], skew_recv.at[me + step])
            pl.when(me > 0)(lambda: skew_copy(me + step, False).start())

    def skew_sent():
        for column in range(columns):
            pl.when((column <= me) & (me + 1 < columns))(lambda: skew_copy(column, True).wait_send())
            pl.when((column >= me) & (me > 0))(lambda: skew_copy(column, False).wait_send())

    norms_line[me] = jnp.full(norms_line.shape[1:], squares, jnp.float32)

    def norm_line_copy(step):
        other = (me + step) % columns
        return remote(
            norms_line.at[me], norms_line.at[me], norm_send.at[0, step], norm_recv.at[0, me], (dp, section, other)
        )

    def norm_plane_copy(step):
        return remote(
            norms_plane.at[row],
            norms_plane.at[row],
            norm_send.at[1, step],
            norm_recv.at[1, row],
            member_id((row + step) % members),
        )

    for step in range(1, columns):
        norm_line_copy(step).start()

    plane_relay(products_kind, tall(products, rows))
    plane_relay(projected_kind, tall(projected, rows))
    for step in range(1, columns):
        other = (me + step) % columns
        landed(norms_line.at[other], norm_recv.at[0, other])
    norms_plane[row] = jnp.sum(norms_line[...], axis=0)
    for step in range(1, members):
        norm_plane_copy(step).start()
    skew_pass(1)
    plane_rest(products_kind, tall(products, rows))
    plane_rest(projected_kind, tall(projected, rows))
    plane_finish(products_kind, tall(products, rows))
    plane_finish(projected_kind, tall(projected, rows))

    def multiply(index, _):
        where = place(index, tile)
        value = product(acts_turned[...], products[:, where]) - product(weights_rows[...], projected[:, where])
        out[:, where] = value
        first[place(row, block), where] = value.astype(HALF)
        return 0

    lax.fori_loop(0, width // tile, multiply, 0)
    plane_start(first_kind, tall(first, block))
    plane_relay(first_kind, tall(first, block))
    for step in range(2, columns - 1):
        skew_pass(step)
    plane_rest(first_kind, tall(first, block))
    skew_pass(columns - 1)
    loads[1].wait()
    for step in range(1, members):
        other = (row + step) % members
        landed(norms_plane.at[other], norm_recv.at[1, other])
    plane_finish(first_kind, tall(first, block))

    mean_square = jnp.sum(norms_plane[...], axis=0)[0:1, 0:1] / (full * full)
    scale = 0.5 * lax.rsqrt(full * (mean_square + 1e-06))
    root = math.sqrt(full)

    def finish(index, _):
        where = place(index, tile)
        value = jnp.zeros((block, tile), jnp.float32)
        for column in range(columns):
            value = value + product(skew[column], first[column * width : (column + 1) * width, where])
        out[:, where] = own[:, where] - (root * scale) * out[:, where] + (0.5 * root * scale * scale) * value
        return 0

    lax.fori_loop(0, width // tile, finish, 0)

    for part in range(parts):
        line_sent(part)
        spread_sent(part)
        for target in range(members):
            pl.when(target != row)(lambda: weights_swap(part, target).wait_send())
    for step in range(1, members):
        acts_swap(step).wait_send()
        norm_plane_copy(step).wait_send()
    for step in range(1, columns):
        norm_line_copy(step).wait_send()
    skew_sent()
    plane_sent(strip_kind, strip)
    plane_sent(acts_kind, tall(acts_columns, rows))
    plane_sent(projected_kind, tall(projected, rows))
    plane_sent(products_kind, tall(products, rows))
    plane_sent(first_kind, tall(first, block))


def run_update(acts, panel, rotation, tokens):
    rows, full = acts.shape
    block, width = rotation.shape
    columns = lax.axis_size("tensor")
    members = lax.axis_size("dp") * lax.axis_size("layer")
    groups, halves = lax.axis_size("dp"), lax.axis_size("layer") // 2
    parts = 2
    kinds = 5
    held = members * rows
    dma = pltpu.SemaphoreType.DMA
    return pl.pallas_call(
        functools.partial(update_kernel, tokens),
        out_shape=jax.ShapeDtypeStruct((block, width), jnp.float32),
        in_specs=[pl.BlockSpec(memory_space=pltpu.VMEM)] + [pl.BlockSpec(memory_space=pl.ANY)] * 2,
        out_specs=pl.BlockSpec(memory_space=pltpu.VMEM),
        scratch_shapes=[
            pltpu.VMEM((full, width), HALF),
            pltpu.VMEM((block, width), jnp.float32),
            pltpu.VMEM((rows, width), HALF),
            pltpu.VMEM((full, rows), HALF),
            pltpu.VMEM((full, rows), HALF),
            pltpu.VMEM((full, rows), HALF),
            pltpu.VMEM((full, rows), HALF),
            pltpu.VMEM((held, width), HALF),
            pltpu.VMEM((held, block), HALF),
            pltpu.VMEM((block, held), HALF),
            pltpu.VMEM((width, held), HALF),
            pltpu.VMEM((block, held), HALF),
            pltpu.VMEM((held, width), HALF),
            pltpu.VMEM((held, width), HALF),
            pltpu.VMEM((rows, width), jnp.float32),
            pltpu.VMEM((columns, block, width), HALF),
            pltpu.VMEM((full, width), HALF),
            pltpu.VMEM((columns, 8, 128), jnp.float32),
            pltpu.VMEM((members, 8, 128), jnp.float32),
            dma((parts, columns, 2)),
            dma((parts, columns, 2)),
            dma((parts, columns, 2)),
            dma((parts, columns)),
            dma((kinds, 2, groups + halves)),
            dma((kinds, 2, groups * halves)),
            dma((kinds, 2, groups, halves)),
            dma((kinds, members, 2)),
            dma((1 + parts, members)),
            dma((1 + parts, members)),
            dma((columns, 2)),
            dma((columns,)),
            dma((2, max(members, columns))),
            dma((2, max(members, columns))),
            dma((2,)),
        ],
        compiler_params=pltpu.CompilerParams(
            collective_id=1, has_side_effects=True, vmem_limit_bytes=62 * 1024 * 1024
        ),
        cost_estimate=pl.CostEstimate(
            flops=2 * full * full * full // 4, bytes_accessed=full * width * 8, transcendentals=0
        ),
    )(acts, panel, rotation)


def shards(embeddings, layer_weight, rotation):
    full = layer_weight.shape[1]
    head = (rotation / math.sqrt(full)).astype(HALF)
    panel = lax.all_gather(head, ROWS, axis=0, tiled=True)
    acts = run_layers(embeddings, layer_weight)
    return run_update(acts, panel, rotation, embeddings.shape[0] * lax.axis_size("dp"))


def solution(mesh):
    return jax.shard_map(
        shards,
        mesh=mesh,
        in_specs=(P("dp", "tensor"), P("layer", None, "tensor"), P(("dp", "layer"), "tensor")),
        out_specs=P(("dp", "layer"), "tensor"),
        check_vma=False,
    )
```

```python
import functools
import math

import jax
import jax.numpy as jnp
from jax import lax
from jax.experimental import pallas as pl
from jax.experimental.pallas import tpu as pltpu
from jax.sharding import PartitionSpec as P

ROWS = ("dp", "layer")
EVERY = ("dp", "layer", "tensor")
HALF = jnp.bfloat16
CHUNKS = 4
LAG = 1
REACH = 2
UPPERS = 1
MESH = pl.DeviceIdType.MESH


def product(left, right, left_dim=1, right_dim=0):
    dims = (((left_dim,), (right_dim,)), ((), ()))
    return lax.dot_general(left, right, dims, preferred_element_type=jnp.float32)


def layers_kernel(
    chunks,
    embeddings,
    weight_hbm,
    records,
    hidden,
    outbox,
    weight,
    update,
    squares,
    send_sem,
    pass_sem,
    recv_sem,
    weight_sem,
):
    dp, section, me = (lax.axis_index(name) for name in EVERY)
    sections, columns = lax.axis_size("layer"), lax.axis_size("tensor")
    levels = weight_hbm.shape[0]
    width = embeddings.shape[1]
    rows = embeddings.shape[0] // chunks
    full = columns * width
    distances = []
    for base in range(0, columns - 1, REACH):
        group = [d for d in range(base + 1, base + REACH + 1) if d < columns]
        distances += group[-1:] + group[:-1] if base + REACH + 1 < columns else group

    loads = [
        pltpu.make_async_copy(weight_hbm.at[level], weight.at[level], weight_sem.at[level])
        for level in range(levels)
    ]
    for load in loads:
        load.start()

    barrier = pltpu.get_barrier_semaphore()

    def greet(row, column):
        pl.semaphore_signal(barrier, inc=1, device_id=(dp, row, column), device_id_type=MESH)

    for column in range(columns):
        pl.when(column != me)(lambda column=column: greet(section, column))
        pl.when(section > 0)(lambda column=column: greet(section - 1, column))
        pl.when(section + 1 < sections)(lambda column=column: greet(section + 1, column))
    edges = jnp.where(section > 0, 1, 0) + jnp.where(section + 1 < sections, 1, 0)
    pl.semaphore_wait(barrier, columns - 1 + columns * edges)

    def remote(source, target, send, recv, row, column):
        return pltpu.make_async_remote_copy(
            src_ref=source,
            dst_ref=target,
            send_sem=send,
            recv_sem=recv,
            device_id=(dp, row, column),
            device_id_type=MESH,
        )

    def own_copy(stage, chunk, offset):
        level, row = (stage, section) if stage < levels else (0, section + 1)
        source = hidden.at[stage, chunk, me] if stage < levels else outbox.at[chunk]
        return remote(
            source,
            hidden.at[level, chunk, me],
            send_sem.at[stage, chunk, offset + REACH],
            recv_sem.at[level, chunk, me],
            row,
            me + offset,
        )

    def own_copies(stage, chunk, action):
        for reach in range(REACH, -1, -1):
            for offset in (reach, -reach) if reach else (0,):
                wanted = (me + offset >= 0) & (me + offset < columns)
                if stage == levels:
                    wanted = wanted & (section + 1 < sections)
                elif offset == 0:
                    continue
                elif stage == 0:
                    wanted = wanted & (section == 0)
                pl.when(wanted)(lambda offset=offset: action(own_copy(stage, chunk, offset)))

    def pass_copy(level, chunk, source, offset):
        view = hidden.at[level, chunk, source]
        return remote(
            view,
            view,
            pass_sem.at[level, chunk, source, abs(offset) - 1],
            recv_sem.at[level, chunk, source],
            section,
            me + offset,
        )

    def passes(level, chunk, distance, way, action):
        if distance % REACH or distance + 1 >= columns:
            return
        source = me - way * distance
        for reach in range(REACH, 0, -1):
            target = me + way * reach
            pl.when((target >= 0) & (target < columns))(
                lambda reach=reach: action(pass_copy(level, chunk, source, way * reach))
            )

    def arrive(level, chunk, source):
        view = hidden.at[level, chunk, source]
        remote(view, view, recv_sem.at[level, chunk, source], recv_sem.at[level, chunk, source], section, me).wait_recv()

    def gather_in(level, chunk, source, first=False):
        value = hidden[level, chunk, source]
        wide = value.astype(jnp.float32)
        square = jnp.sum(wide * wide, axis=-1, keepdims=True)
        part = product(value, weight[level, pl.ds(pl.multiple_of(source * width, width), width), :])
        squares[...] = square if first else squares[...] + square
        update[...] = part if first else update[...] + part

    def step(level, chunk):
        if level == 0:
            pl.when(section > 0)(lambda: arrive(level, chunk, me))
        gather_in(level, chunk, me, True)
        for distance in distances:
            for way in (1, -1):
                source = me - way * distance

                @pl.when((source >= 0) & (source < columns))
                def _():
                    arrive(level, chunk, source)
                    passes(level, chunk, distance, way, lambda one: one.start())
                    gather_in(level, chunk, source)

        inverse = lax.rsqrt(squares[...] / full + 1e-05)
        fresh = (hidden[level, chunk, me].astype(jnp.float32) + inverse * update[...]).astype(HALF)
        if level + 1 < levels:
            hidden[level + 1, chunk, me] = fresh
        else:
            outbox[chunk] = fresh
        own_copies(level + 1, chunk, lambda one: one.start())
        for column in range(columns):
            wide = hidden[level, chunk, column].astype(jnp.float32)
            records[level, chunk, :, column * width : (column + 1) * width] = (wide * inverse).astype(HALF)

    @pl.when(section == 0)
    def _():
        for chunk in range(chunks):
            hidden[0, chunk, me] = embeddings[chunk * rows : (chunk + 1) * rows, :]

    for chunk in range(chunks):
        own_copies(0, chunk, lambda one: one.start())

    def turn(index, _):
        for level in range(levels):
            chunk = index - level * LAG

            @pl.when((chunk >= 0) & (chunk < chunks))
            def _():
                pl.when(chunk == 0)(lambda: loads[level].wait())
                step(level, chunk)

        return 0

    lax.fori_loop(0, chunks + (levels - 1) * LAG, turn, 0)

    for chunk in range(chunks):
        for stage in range(levels + 1):
            own_copies(stage, chunk, lambda one: one.wait_send())
        for level in range(levels):
            for distance in distances:
                for way in (1, -1):
                    source = me - way * distance
                    pl.when((source >= 0) & (source < columns))(
                        lambda distance=distance, way=way: passes(
                            level, chunk, distance, way, lambda one: one.wait_send()
                        )
                    )


def run_layers(embeddings, layer_weight):
    levels, full, width = layer_weight.shape
    tokens = embeddings.shape[0]
    columns = lax.axis_size("tensor")
    rows = tokens // CHUNKS
    dma = pltpu.SemaphoreType.DMA
    records = pl.pallas_call(
        functools.partial(layers_kernel, CHUNKS),
        out_shape=jax.ShapeDtypeStruct((levels, CHUNKS, rows, full), HALF),
        in_specs=[pl.BlockSpec(memory_space=pltpu.VMEM), pl.BlockSpec(memory_space=pl.ANY)],
        out_specs=pl.BlockSpec(memory_space=pltpu.VMEM),
        scratch_shapes=[
            pltpu.VMEM((levels, CHUNKS, columns, rows, width), HALF),
            pltpu.VMEM((CHUNKS, rows, width), HALF),
            pltpu.VMEM((levels, full, width), HALF),
            pltpu.VMEM((rows, width), jnp.float32),
            pltpu.VMEM((rows, 1), jnp.float32),
            dma((levels + 1, CHUNKS, 2 * REACH + 1)),
            dma((levels, CHUNKS, columns, REACH)),
            dma((levels, CHUNKS, columns)),
            dma((levels,)),
        ],
        compiler_params=pltpu.CompilerParams(
            collective_id=0, has_side_effects=True, vmem_limit_bytes=40 * 1024 * 1024
        ),
        cost_estimate=pl.CostEstimate(
            flops=2 * tokens * full * width * levels * 40,
            bytes_accessed=layer_weight.size * 2 * 20,
            transcendentals=0,
        ),
    )(embeddings, layer_weight)
    return records.reshape(levels * tokens, full)


def update_kernel(
    tokens,
    acts_hbm,
    panel_hbm,
    own_hbm,
    out,
    acts,
    panel,
    own,
    cubes,
    partial,
    from_left,
    from_right,
    weights,
    acts_columns,
    acts_rows,
    acts_turned,
    weights_columns,
    weights_rows,
    projected,
    products,
    total,
    skew,
    first,
    norms_line,
    norms_plane,
    line_send,
    line_recv,
    spread_send,
    spread_recv,
    plane_send,
    plane_pass,
    plane_cross,
    plane_recv,
    swap_send,
    swap_recv,
    skew_send,
    skew_recv,
    norm_send,
    norm_recv,
    load_sem,
):
    dp, section, me = (lax.axis_index(name) for name in EVERY)
    groups, sections, columns = (lax.axis_size(name) for name in EVERY)
    loads = [
        pltpu.make_async_copy(panel_hbm, panel, load_sem.at[0]),
        pltpu.make_async_copy(own_hbm, own, load_sem.at[1]),
        pltpu.make_async_copy(acts_hbm, acts, load_sem.at[2]),
    ]
    for load in (loads[2], loads[0], loads[1]):
        load.start()
    rows, full = acts_hbm.shape
    block, width = own_hbm.shape
    members = groups * sections
    halves = sections // 2
    core = section % 2
    side = section // 2
    row = dp * sections + section
    tile = min(256, width)
    parts = 2
    part_rows = rows // parts
    per_column = width // block

    def place(index, size):
        return pl.ds(pl.multiple_of(index * size, size), size)

    def member_id(index):
        return (index // sections, index % sections, me)

    def at(across, along, which):
        return (dp + across) % groups, ((side + along) % halves) * 2 + which

    def index_of(spot):
        return spot[0] * sections + spot[1]

    def remote(source, target, send, recv, device):
        return pltpu.make_async_remote_copy(
            src_ref=source, dst_ref=target, send_sem=send, recv_sem=recv, device_id=device, device_id_type=MESH
        )

    def landed(target, recv):
        remote(target, target, recv, recv, (dp, section, me)).wait_recv()

    barrier = pltpu.get_barrier_semaphore()
    for step in range(1, members):
        pl.semaphore_signal(barrier, inc=1, device_id=member_id((row + step) % members), device_id_type=MESH)
    for step in range(1, columns):
        pl.semaphore_signal(barrier, inc=1, device_id=(dp, section, (me + step) % columns), device_id_type=MESH)
    pl.semaphore_wait(barrier, members - 1 + columns - 1)

    def send_to(view, source, half, spot, send, kind):
        piece = view(source, half)
        return remote(piece, piece, send, plane_recv.at[kind, source, half], (spot[0], spot[1], me))

    def plane_copies(kind, view, which=(0, 1)):
        def across(half):
            return [
                send_to(view, row, half, at(x, 0, core), plane_send.at[kind, half, x], kind) for x in range(1, groups)
            ]

        def along(half):
            return [
                send_to(view, row, half, at(0, y, core), plane_send.at[kind, half, groups + y], kind)
                for y in range(1, halves)
            ]

        def other(half):
            return [send_to(view, row, half, at(0, 0, 1 - core), plane_send.at[kind, half, 0], kind)]

        return [
            along(half) + across(half) + other(half) if half else across(half) + along(half) + other(half)
            for half in which
        ]

    def pass_copies(kind, view, x, y, half):
        source = index_of(at(x, y, core))
        copies = []
        if half == 0 and y == 0:
            copies += [
                send_to(view, source, half, at(0, z, core), plane_cross.at[kind, half, x, z], kind)
                for z in range(1, halves)
            ]
        if half == 1 and x == 0:
            copies += [
                send_to(view, source, half, at(z, 0, core), plane_cross.at[kind, half, z, y], kind)
                for z in range(1, groups)
            ]
        copies.append(send_to(view, source, half, at(0, 0, 1 - core), plane_pass.at[kind, half, x * halves + y], kind))
        return source, copies

    def plane_start(kind, view, which=(0, 1)):
        copies = plane_copies(kind, view, which)
        most = max(len(one) for one in copies)
        for spot in range(most):
            for one in copies:
                if spot < len(one):
                    one[spot].start()

    near = [(x, 0) for x in range(1, groups)]
    beside = [(0, y) for y in range(1, halves)]
    beyond = [(x, y) for x in range(1, groups) for y in range(1, halves)]

    def plane_take(kind, view, spots, half):
        for x, y in spots:
            source, copies = pass_copies(kind, view, x, y, half)
            landed(view(source, half), plane_recv.at[kind, source, half])
            for one in copies:
                one.start()

    def plane_relay(kind, view):
        plane_take(kind, view, near, 0)
        plane_take(kind, view, beside, 1)

    def plane_rest(kind, view):
        plane_take(kind, view, near, 1)
        plane_take(kind, view, beside, 0)
        for half in range(2):
            plane_take(kind, view, beyond, half)

    def plane_finish(kind, view):
        for x in range(groups):
            for y in range(halves):
                source = index_of(at(x, y, 1 - core))
                for half in range(2):
                    landed(view(source, half), plane_recv.at[kind, source, half])

    def plane_sent(kind, view):
        for copies in plane_copies(kind, view):
            for one in copies:
                one.wait_send()
        for half in range(2):
            for x, y in near + beside + beyond:
                for one in pass_copies(kind, view, x, y, half)[1]:
                    one.wait_send()

    def tall(ref, size):
        return lambda index, half: ref.at[place(2 * index + half, size // 2)]

    def strip(index, half):
        return weights_columns.at[:, place(2 * index + half, part_rows)]

    acts_kind, projected_kind, products_kind, first_kind, strip_kind = 0, 1, 2, 3, 4

    loads[2].wait()
    acts_columns[place(row, rows)] = acts[:, place(me, width)]
    plane_start(acts_kind, tall(acts_columns, rows))

    def acts_swap(step):
        target = (row + step) % members
        return remote(
            acts.at[:, place(target, block)],
            acts_rows.at[place(row, rows)],
            swap_send.at[0, step],
            swap_recv.at[0, row],
            member_id(target),
        )

    acts_rows[place(row, rows)] = acts[:, place(row, block)]
    loads[0].wait()

    def project(index, _):
        where = place(index, tile)
        value = product(acts[...], panel[:, where])
        projected[place(row, rows), where] = value.astype(HALF)
        cubes[:, where] = (value * value * value * (1.0 / tokens)).astype(HALF)
        return 0

    lax.fori_loop(0, width // tile, project, 0)
    plane_relay(acts_kind, tall(acts_columns, rows))
    for step in range(1, members):
        acts_swap(step).start()

    def piece(ref, column, part):
        return ref.at[place(column, width), place(part, part_rows)]

    def line_copy(part, column, right, source):
        target = from_left if right else from_right
        way = 0 if right else 1
        return remote(
            piece(source, column, part),
            piece(target, column, part),
            line_send.at[part, column, way],
            line_recv.at[part, column, way],
            (dp, section, me + 1 if right else me - 1),
        )

    def add_into(target, column, part):
        lanes = place(part, part_rows)

        def one(index, _):
            where = place(column * (width // tile) + index, tile)
            target[where, lanes] = (
                target[where, lanes].astype(jnp.float32) + partial[where, lanes].astype(jnp.float32)
            ).astype(HALF)
            return 0

        lax.fori_loop(0, width // tile, one, 0)

    def first_sends(part, steps):
        for step in steps:
            right, left = columns - 1 - step, step
            pl.when(me == 0)(lambda: line_copy(part, right, True, partial).start())
            pl.when(me == columns - 1)(lambda: line_copy(part, left, False, partial).start())

    def relay_right(part, step):
        column = columns - 1 - step

        @pl.when((me > 0) & (me < column))
        def _():
            landed(piece(from_left, column, part), line_recv.at[part, column, 0])
            add_into(from_left, column, part)
            line_copy(part, column, True, from_left).start()

    def relay_left(part, step):
        column = step

        @pl.when((me < columns - 1) & (me > column))
        def _():
            landed(piece(from_right, column, part), line_recv.at[part, column, 1])
            add_into(from_right, column, part)
            line_copy(part, column, False, from_right).start()

    def relay(part, step):
        pl.when(me < columns // 2)(lambda: relay_right(part, step))
        relay_left(part, step)
        pl.when(me >= columns // 2)(lambda: relay_right(part, step))

    def line_sent(part):
        for column in range(columns):
            pl.when(me < column)(lambda: line_copy(part, column, True, partial).wait_send())
            pl.when(me > column)(lambda: line_copy(part, column, False, partial).wait_send())

    def settle(part):
        lanes = place(part, part_rows)
        pl.when(me > 0)(lambda: landed(piece(from_left, me, part), line_recv.at[part, me, 0]))
        pl.when(me < columns - 1)(lambda: landed(piece(from_right, me, part), line_recv.at[part, me, 1]))
        left = jnp.where(me > 0, 1.0, 0.0)
        right = jnp.where(me < columns - 1, 1.0, 0.0)

        def one(index, _):
            where = place(me * (width // tile) + index, tile)
            value = partial[where, lanes].astype(jnp.float32)
            value = value + jnp.where(left > 0.5, from_left[where, lanes].astype(jnp.float32), 0.0)
            value = value + jnp.where(right > 0.5, from_right[where, lanes].astype(jnp.float32), 0.0)
            final = value.astype(HALF)
            weights[where, lanes] = final
            weights_columns[place(index, tile), place(row * parts + part, part_rows)] = final
            return 0

        lax.fori_loop(0, width // tile, one, 0)

    def spread_copy(part, column, right):
        view = piece(weights, column, part)
        return remote(
            view,
            view,
            spread_send.at[part, column, 0 if right else 1],
            spread_recv.at[part, column],
            (dp, section, me + 1 if right else me - 1),
        )

    def weights_swap(part, target):
        return remote(
            weights.at[place(target, block), place(part, part_rows)],
            weights_rows.at[:, place(row * parts + part, part_rows)],
            swap_send.at[1 + part, target],
            swap_recv.at[1 + part, row],
            member_id(target),
        )

    def hand_out(part, column):
        for index in range(per_column):
            target = column * per_column + index
            pl.when(target != row)(lambda: weights_swap(part, target).start())

            @pl.when(target == row)
            def _():
                weights_rows[:, place(row * parts + part, part_rows)] = weights[
                    place(row, block), place(part, part_rows)
                ]

    def offer(part):
        pl.when(me + 1 < columns)(lambda: spread_copy(part, me, True).start())
        pl.when(me > 0)(lambda: spread_copy(part, me, False).start())
        plane_start(strip_kind, strip, (part,))
        hand_out(part, me)

    def spread(part, step):
        @pl.when(me >= step)
        def _():
            landed(piece(weights, me - step, part), spread_recv.at[part, me - step])
            pl.when(me + 1 < columns)(lambda: spread_copy(part, me - step, True).start())
            hand_out(part, me - step)

        @pl.when(me + step < columns)
        def _():
            landed(piece(weights, me + step, part), spread_recv.at[part, me + step])
            pl.when(me > 0)(lambda: spread_copy(part, me + step, False).start())
            hand_out(part, me + step)

    def spread_sent(part):
        for column in range(columns):
            pl.when((column <= me) & (me + 1 < columns))(lambda: spread_copy(part, column, True).wait_send())
            pl.when((column >= me) & (me > 0))(lambda: spread_copy(part, column, False).wait_send())

    steps = range(columns - 1)

    def weigh(index, _):
        where = place(jnp.where(me < columns // 2, columns - 1 - index, index), width)
        partial[where] = product(panel[where], cubes[...], 1, 1).astype(HALF)
        return 0

    for step in steps:
        weigh(step, 0)
        first_sends(0, [step])
    weigh(columns - 1, 0)
    first_sends(1, steps[:1])
    for step in steps:
        relay(0, step)
    settle(0)
    offer(0)
    first_sends(1, steps[1:])
    for step in steps:
        relay(1, step)
        spread(0, step + 1)
    settle(1)
    offer(1)
    plane_take(strip_kind, strip, near, 0)
    plane_rest(acts_kind, tall(acts_columns, rows))
    for other in range(1, members):
        source = (row + other) % members
        landed(acts_rows.at[place(source, rows)], swap_recv.at[0, source])

    def turn(index, _):
        acts_turned[:, place(index, rows)] = acts_rows[place(index, rows)].T
        return 0

    for step in steps:
        spread(1, step + 1)
        if step == 0:
            plane_take(strip_kind, strip, beside, 1)
    lax.fori_loop(0, members, turn, 0)

    def apply(index, _):
        where = place(index, width)
        total[...] += product(weights[where], panel[where], 0, 0)
        return 0

    total[...] = jnp.zeros_like(total)
    lax.fori_loop(0, columns, apply, 0)
    products[place(row, rows)] = total[...].astype(HALF)
    plane_start(products_kind, tall(products, rows))
    plane_start(projected_kind, tall(projected, rows))

    plane_rest(strip_kind, strip)
    plane_finish(acts_kind, tall(acts_columns, rows))
    for part in range(parts):
        for other in range(1, members):
            source = (row + other) % members
            landed(weights_rows.at[:, place(source * parts + part, part_rows)], swap_recv.at[1 + part, source])
    plane_finish(strip_kind, strip)

    def build(index, squares):
        where = place(index, tile)
        value = product(acts_turned[...], weights_columns[where], 1, 1) - product(
            weights_rows[...], acts_columns[:, where]
        )
        skew[me, :, where] = value.astype(HALF)
        return squares + jnp.sum(value * value)

    squares = lax.fori_loop(0, width // tile, build, jnp.float32(0.0))

    def skew_copy(column, right):
        view = skew.at[column]
        return remote(
            view,
            view,
            skew_send.at[column, 0 if right else 1],
            skew_recv.at[column],
            (dp, section, me + 1 if right else me - 1),
        )

    pl.when(me + 1 < columns)(lambda: skew_copy(me, True).start())
    pl.when(me > 0)(lambda: skew_copy(me, False).start())

    def skew_pass(step):
        @pl.when(me >= step)
        def _():
            landed(skew.at[me - step], skew_recv.at[me - step])
            pl.when(me + 1 < columns)(lambda: skew_copy(me - step, True).start())

        @pl.when(me + step < columns)
        def _():
            landed(skew.at[me + step], skew_recv.at[me + step])
            pl.when(me > 0)(lambda: skew_copy(me + step, False).start())

    def skew_sent():
        for column in range(columns):
            pl.when((column <= me) & (me + 1 < columns))(lambda: skew_copy(column, True).wait_send())
            pl.when((column >= me) & (me > 0))(lambda: skew_copy(column, False).wait_send())

    norms_line[me] = jnp.full(norms_line.shape[1:], squares, jnp.float32)

    def norm_line_copy(step):
        other = (me + step) % columns
        return remote(
            norms_line.at[me], norms_line.at[me], norm_send.at[0, step], norm_recv.at[0, me], (dp, section, other)
        )

    def norm_plane_copy(step):
        return remote(
            norms_plane.at[row],
            norms_plane.at[row],
            norm_send.at[1, step],
            norm_recv.at[1, row],
            member_id((row + step) % members),
        )

    for step in range(1, columns):
        norm_line_copy(step).start()

    plane_relay(products_kind, tall(products, rows))
    plane_relay(projected_kind, tall(projected, rows))
    for step in range(1, columns):
        other = (me + step) % columns
        landed(norms_line.at[other], norm_recv.at[0, other])
    norms_plane[row] = jnp.sum(norms_line[...], axis=0)
    for step in range(1, members):
        norm_plane_copy(step).start()
    skew_pass(1)
    plane_rest(products_kind, tall(products, rows))
    plane_rest(projected_kind, tall(projected, rows))
    plane_finish(products_kind, tall(products, rows))
    plane_finish(projected_kind, tall(projected, rows))

    for half in range(2):
        lines = slice(half * (block // 2), (half + 1) * (block // 2))

        def multiply(index, _):
            where = place(index, tile)
            value = product(acts_turned[lines], products[:, where]) - product(weights_rows[lines], projected[:, where])
            out[lines, where] = value
            first[place(2 * row + half, block // 2), where] = value.astype(HALF)
            return 0

        lax.fori_loop(0, width // tile, multiply, 0)
        plane_start(first_kind, tall(first, block), (half,))
    for step in range(2, columns - 1):
        skew_pass(step)
    plane_relay(first_kind, tall(first, block))
    plane_rest(first_kind, tall(first, block))
    skew_pass(columns - 1)
    loads[1].wait()
    for step in range(1, members):
        other = (row + step) % members
        landed(norms_plane.at[other], norm_recv.at[1, other])
    plane_finish(first_kind, tall(first, block))

    mean_square = jnp.sum(norms_plane[...], axis=0)[0:1, 0:1] / (full * full)
    scale = 0.5 * lax.rsqrt(full * (mean_square + 1e-06))
    root = math.sqrt(full)

    def finish(index, _):
        where = place(index, tile)
        value = jnp.zeros((block, tile), jnp.float32)
        for column in range(columns):
            value = value + product(skew[column], first[column * width : (column + 1) * width, where])
        out[:, where] = own[:, where] - (root * scale) * out[:, where] + (0.5 * root * scale * scale) * value
        return 0

    lax.fori_loop(0, width // tile, finish, 0)

    for part in range(parts):
        line_sent(part)
        spread_sent(part)
        for target in range(members):
            pl.when(target != row)(lambda: weights_swap(part, target).wait_send())
    for step in range(1, members):
        acts_swap(step).wait_send()
        norm_plane_copy(step).wait_send()
    for step in range(1, columns):
        norm_line_copy(step).wait_send()
    skew_sent()
    plane_sent(strip_kind, strip)
    plane_sent(acts_kind, tall(acts_columns, rows))
    plane_sent(projected_kind, tall(projected, rows))
    plane_sent(products_kind, tall(products, rows))
    plane_sent(first_kind, tall(first, block))


def run_update(acts, panel, rotation, tokens):
    rows, full = acts.shape
    block, width = rotation.shape
    columns = lax.axis_size("tensor")
    members = lax.axis_size("dp") * lax.axis_size("layer")
    groups, halves = lax.axis_size("dp"), lax.axis_size("layer") // 2
    parts = 2
    kinds = 5
    held = members * rows
    dma = pltpu.SemaphoreType.DMA
    return pl.pallas_call(
        functools.partial(update_kernel, tokens),
        out_shape=jax.ShapeDtypeStruct((block, width), jnp.float32),
        in_specs=[pl.BlockSpec(memory_space=pl.ANY)] * 3,
        out_specs=pl.BlockSpec(memory_space=pltpu.VMEM),
        scratch_shapes=[
            pltpu.VMEM((rows, full), HALF),
            pltpu.VMEM((full, width), HALF),
            pltpu.VMEM((block, width), jnp.float32),
            pltpu.VMEM((rows, width), HALF),
            pltpu.VMEM((full, rows), HALF),
            pltpu.VMEM((full, rows), HALF),
            pltpu.VMEM((full, rows), HALF),
            pltpu.VMEM((full, rows), HALF),
            pltpu.VMEM((held, width), HALF),
            pltpu.VMEM((held, block), HALF),
            pltpu.VMEM((block, held), HALF),
            pltpu.VMEM((width, held), HALF),
            pltpu.VMEM((block, held), HALF),
            pltpu.VMEM((held, width), HALF),
            pltpu.VMEM((held, width), HALF),
            pltpu.VMEM((rows, width), jnp.float32),
            pltpu.VMEM((columns, block, width), HALF),
            pltpu.VMEM((full, width), HALF),
            pltpu.VMEM((columns, 8, 128), jnp.float32),
            pltpu.VMEM((members, 8, 128), jnp.float32),
            dma((parts, columns, 2)),
            dma((parts, columns, 2)),
            dma((parts, columns, 2)),
            dma((parts, columns)),
            dma((kinds, 2, groups + halves)),
            dma((kinds, 2, groups * halves)),
            dma((kinds, 2, groups, halves)),
            dma((kinds, members, 2)),
            dma((1 + parts, members)),
            dma((1 + parts, members)),
            dma((columns, 2)),
            dma((columns,)),
            dma((2, max(members, columns))),
            dma((2, max(members, columns))),
            dma((3,)),
        ],
        compiler_params=pltpu.CompilerParams(
            collective_id=1, has_side_effects=True, vmem_limit_bytes=62 * 1024 * 1024
        ),
        cost_estimate=pl.CostEstimate(
            flops=2 * full * full * full // 4, bytes_accessed=full * width * 8, transcendentals=0
        ),
    )(acts, panel, rotation)


def shards(embeddings, layer_weight, rotation):
    full = layer_weight.shape[1]
    head = (rotation / math.sqrt(full)).astype(HALF)
    panel = lax.all_gather(head, ROWS, axis=0, tiled=True)
    acts = run_layers(embeddings, layer_weight)
    return run_update(acts, panel, rotation, embeddings.shape[0] * lax.axis_size("dp"))


def solution(mesh):
    return jax.shard_map(
        shards,
        mesh=mesh,
        in_specs=(P("dp", "tensor"), P("layer", None, "tensor"), P(("dp", "layer"), "tensor")),
        out_specs=P(("dp", "layer"), "tensor"),
        check_vma=False,
    )
```

```python
import functools
import math

import jax
import jax.numpy as jnp
from jax import lax
from jax.experimental import pallas as pl
from jax.experimental.pallas import tpu as pltpu
from jax.sharding import PartitionSpec as P

ROWS = ("dp", "layer")
EVERY = ("dp", "layer", "tensor")
HALF = jnp.bfloat16
CHUNKS = 4
LAG = 1
REACH = 2
UPPERS = 1
MESH = pl.DeviceIdType.MESH


def product(left, right, left_dim=1, right_dim=0):
    dims = (((left_dim,), (right_dim,)), ((), ()))
    return lax.dot_general(left, right, dims, preferred_element_type=jnp.float32)


def layers_kernel(
    chunks,
    embeddings,
    weight_hbm,
    records,
    hidden,
    outbox,
    weight,
    update,
    squares,
    send_sem,
    pass_sem,
    recv_sem,
    weight_sem,
):
    dp, section, me = (lax.axis_index(name) for name in EVERY)
    sections, columns = lax.axis_size("layer"), lax.axis_size("tensor")
    levels = weight_hbm.shape[0]
    width = embeddings.shape[1]
    rows = embeddings.shape[0] // chunks
    full = columns * width
    distances = []
    for base in range(0, columns - 1, REACH):
        group = [d for d in range(base + 1, base + REACH + 1) if d < columns]
        distances += group[-1:] + group[:-1] if base + REACH + 1 < columns else group

    loads = [
        pltpu.make_async_copy(weight_hbm.at[level], weight.at[level], weight_sem.at[level])
        for level in range(levels)
    ]
    loads[0].start()

    barrier = pltpu.get_barrier_semaphore()

    def greet(row, column):
        pl.semaphore_signal(barrier, inc=1, device_id=(dp, row, column), device_id_type=MESH)

    for column in range(columns):
        pl.when(column != me)(lambda column=column: greet(section, column))
        pl.when(section > 0)(lambda column=column: greet(section - 1, column))
        pl.when(section + 1 < sections)(lambda column=column: greet(section + 1, column))
    edges = jnp.where(section > 0, 1, 0) + jnp.where(section + 1 < sections, 1, 0)
    pl.semaphore_wait(barrier, columns - 1 + columns * edges)
    for load in loads[1:]:
        load.start()

    def remote(source, target, send, recv, row, column):
        return pltpu.make_async_remote_copy(
            src_ref=source,
            dst_ref=target,
            send_sem=send,
            recv_sem=recv,
            device_id=(dp, row, column),
            device_id_type=MESH,
        )

    def own_copy(stage, chunk, offset):
        level, row = (stage, section) if stage < levels else (0, section + 1)
        source = hidden.at[stage, chunk, me] if stage < levels else outbox.at[chunk]
        return remote(
            source,
            hidden.at[level, chunk, me],
            send_sem.at[stage, chunk, offset + REACH],
            recv_sem.at[level, chunk, me],
            row,
            me + offset,
        )

    def own_copies(stage, chunk, action):
        for reach in range(REACH, -1, -1):
            for offset in (reach, -reach) if reach else (0,):
                wanted = (me + offset >= 0) & (me + offset < columns)
                if stage == levels:
                    wanted = wanted & (section + 1 < sections)
                elif offset == 0:
                    continue
                elif stage == 0:
                    wanted = wanted & (section == 0)
                pl.when(wanted)(lambda offset=offset: action(own_copy(stage, chunk, offset)))

    def pass_copy(level, chunk, source, offset):
        view = hidden.at[level, chunk, source]
        return remote(
            view,
            view,
            pass_sem.at[level, chunk, source, abs(offset) - 1],
            recv_sem.at[level, chunk, source],
            section,
            me + offset,
        )

    def passes(level, chunk, distance, way, action):
        if distance % REACH or distance + 1 >= columns:
            return
        source = me - way * distance
        for reach in range(REACH, 0, -1):
            target = me + way * reach
            pl.when((target >= 0) & (target < columns))(
                lambda reach=reach: action(pass_copy(level, chunk, source, way * reach))
            )

    def arrive(level, chunk, source):
        view = hidden.at[level, chunk, source]
        remote(view, view, recv_sem.at[level, chunk, source], recv_sem.at[level, chunk, source], section, me).wait_recv()

    def gather_in(level, chunk, source, first=False):
        value = hidden[level, chunk, source]
        wide = value.astype(jnp.float32)
        square = jnp.sum(wide * wide, axis=-1, keepdims=True)
        part = product(value, weight[level, pl.ds(pl.multiple_of(source * width, width), width), :])
        squares[...] = square if first else squares[...] + square
        update[...] = part if first else update[...] + part

    def step(level, chunk):
        if level == 0:
            pl.when(section > 0)(lambda: arrive(level, chunk, me))
        gather_in(level, chunk, me, True)
        for distance in distances:
            for way in (1, -1):
                source = me - way * distance

                @pl.when((source >= 0) & (source < columns))
                def _():
                    arrive(level, chunk, source)
                    passes(level, chunk, distance, way, lambda one: one.start())
                    gather_in(level, chunk, source)

        inverse = lax.rsqrt(squares[...] / full + 1e-05)
        fresh = (hidden[level, chunk, me].astype(jnp.float32) + inverse * update[...]).astype(HALF)
        if level + 1 < levels:
            hidden[level + 1, chunk, me] = fresh
        else:
            outbox[chunk] = fresh
        own_copies(level + 1, chunk, lambda one: one.start())
        for column in range(columns):
            wide = hidden[level, chunk, column].astype(jnp.float32)
            records[level, chunk, :, column * width : (column + 1) * width] = (wide * inverse).astype(HALF)

    @pl.when(section == 0)
    def _():
        for chunk in range(chunks):
            hidden[0, chunk, me] = embeddings[chunk * rows : (chunk + 1) * rows, :]

    for chunk in range(chunks):
        own_copies(0, chunk, lambda one: one.start())

    def turn(index, _):
        for level in range(levels):
            chunk = index - level * LAG

            @pl.when((chunk >= 0) & (chunk < chunks))
            def _():
                pl.when(chunk == 0)(lambda: loads[level].wait())
                step(level, chunk)

        return 0

    lax.fori_loop(0, chunks + (levels - 1) * LAG, turn, 0)

    for chunk in range(chunks):
        for stage in range(levels + 1):
            own_copies(stage, chunk, lambda one: one.wait_send())
        for level in range(levels):
            for distance in distances:
                for way in (1, -1):
                    source = me - way * distance
                    pl.when((source >= 0) & (source < columns))(
                        lambda distance=distance, way=way: passes(
                            level, chunk, distance, way, lambda one: one.wait_send()
                        )
                    )


def run_layers(embeddings, layer_weight):
    levels, full, width = layer_weight.shape
    tokens = embeddings.shape[0]
    columns = lax.axis_size("tensor")
    rows = tokens // CHUNKS
    dma = pltpu.SemaphoreType.DMA
    records = pl.pallas_call(
        functools.partial(layers_kernel, CHUNKS),
        out_shape=jax.ShapeDtypeStruct((levels, CHUNKS, rows, full), HALF),
        in_specs=[pl.BlockSpec(memory_space=pltpu.VMEM), pl.BlockSpec(memory_space=pl.ANY)],
        out_specs=pl.BlockSpec(memory_space=pltpu.VMEM),
        scratch_shapes=[
            pltpu.VMEM((levels, CHUNKS, columns, rows, width), HALF),
            pltpu.VMEM((CHUNKS, rows, width), HALF),
            pltpu.VMEM((levels, full, width), HALF),
            pltpu.VMEM((rows, width), jnp.float32),
            pltpu.VMEM((rows, 1), jnp.float32),
            dma((levels + 1, CHUNKS, 2 * REACH + 1)),
            dma((levels, CHUNKS, columns, REACH)),
            dma((levels, CHUNKS, columns)),
            dma((levels,)),
        ],
        compiler_params=pltpu.CompilerParams(
            collective_id=0, has_side_effects=True, vmem_limit_bytes=40 * 1024 * 1024
        ),
        cost_estimate=pl.CostEstimate(
            flops=2 * tokens * full * width * levels * 40,
            bytes_accessed=layer_weight.size * 2 * 20,
            transcendentals=0,
        ),
    )(embeddings, layer_weight)
    return records.reshape(levels * tokens, full)


def update_kernel(
    tokens,
    acts_hbm,
    panel_hbm,
    own_hbm,
    out,
    acts,
    panel,
    own,
    cubes,
    partial,
    from_left,
    from_right,
    weights,
    acts_columns,
    acts_rows,
    acts_turned,
    weights_columns,
    weights_rows,
    projected,
    products,
    total,
    skew,
    first,
    norms_line,
    norms_plane,
    line_send,
    line_recv,
    spread_send,
    spread_recv,
    plane_send,
    plane_pass,
    plane_cross,
    plane_recv,
    swap_send,
    swap_recv,
    skew_send,
    skew_recv,
    norm_send,
    norm_recv,
    load_sem,
):
    dp, section, me = (lax.axis_index(name) for name in EVERY)
    groups, sections, columns = (lax.axis_size(name) for name in EVERY)
    loads = [
        pltpu.make_async_copy(panel_hbm, panel, load_sem.at[0]),
        pltpu.make_async_copy(own_hbm, own, load_sem.at[1]),
        pltpu.make_async_copy(acts_hbm, acts, load_sem.at[2]),
    ]
    for load in (loads[2], loads[0], loads[1]):
        load.start()
    rows, full = acts_hbm.shape
    block, width = own_hbm.shape
    members = groups * sections
    halves = sections // 2
    core = section % 2
    side = section // 2
    row = dp * sections + section
    tile = min(256, width)
    parts = 2
    part_rows = rows // parts
    per_column = width // block

    def place(index, size):
        return pl.ds(pl.multiple_of(index * size, size), size)

    def member_id(index):
        return (index // sections, index % sections, me)

    def at(across, along, which):
        return (dp + across) % groups, ((side + along) % halves) * 2 + which

    def index_of(spot):
        return spot[0] * sections + spot[1]

    def remote(source, target, send, recv, device):
        return pltpu.make_async_remote_copy(
            src_ref=source, dst_ref=target, send_sem=send, recv_sem=recv, device_id=device, device_id_type=MESH
        )

    def landed(target, recv):
        remote(target, target, recv, recv, (dp, section, me)).wait_recv()

    barrier = pltpu.get_barrier_semaphore()
    for step in range(1, members):
        pl.semaphore_signal(barrier, inc=1, device_id=member_id((row + step) % members), device_id_type=MESH)
    for step in range(1, columns):
        pl.semaphore_signal(barrier, inc=1, device_id=(dp, section, (me + step) % columns), device_id_type=MESH)
    pl.semaphore_wait(barrier, members - 1 + columns - 1)

    def send_to(view, source, half, spot, send, kind):
        piece = view(source, half)
        return remote(piece, piece, send, plane_recv.at[kind, source, half], (spot[0], spot[1], me))

    def plane_copies(kind, view, which=(0, 1)):
        def across(half):
            return [
                send_to(view, row, half, at(x, 0, core), plane_send.at[kind, half, x], kind) for x in range(1, groups)
            ]

        def along(half):
            return [
                send_to(view, row, half, at(0, y, core), plane_send.at[kind, half, groups + y], kind)
                for y in range(1, halves)
            ]

        def other(half):
            return [send_to(view, row, half, at(0, 0, 1 - core), plane_send.at[kind, half, 0], kind)]

        return [
            along(half) + across(half) + other(half) if half else across(half) + along(half) + other(half)
            for half in which
        ]

    def pass_copies(kind, view, x, y, half):
        source = index_of(at(x, y, core))
        copies = []
        if half == 0 and y == 0:
            copies += [
                send_to(view, source, half, at(0, z, core), plane_cross.at[kind, half, x, z], kind)
                for z in range(1, halves)
            ]
        if half == 1 and x == 0:
            copies += [
                send_to(view, source, half, at(z, 0, core), plane_cross.at[kind, half, z, y], kind)
                for z in range(1, groups)
            ]
        copies.append(send_to(view, source, half, at(0, 0, 1 - core), plane_pass.at[kind, half, x * halves + y], kind))
        return source, copies

    def plane_start(kind, view, which=(0, 1)):
        copies = plane_copies(kind, view, which)
        most = max(len(one) for one in copies)
        for spot in range(most):
            for one in copies:
                if spot < len(one):
                    one[spot].start()

    near = [(x, 0) for x in range(1, groups)]
    beside = [(0, y) for y in range(1, halves)]
    beyond = [(x, y) for x in range(1, groups) for y in range(1, halves)]

    def plane_take(kind, view, spots, half):
        for x, y in spots:
            source, copies = pass_copies(kind, view, x, y, half)
            landed(view(source, half), plane_recv.at[kind, source, half])
            for one in copies:
                one.start()

    def plane_relay(kind, view):
        plane_take(kind, view, near, 0)
        plane_take(kind, view, beside, 1)

    def plane_rest(kind, view):
        plane_take(kind, view, near, 1)
        plane_take(kind, view, beside, 0)
        for half in range(2):
            plane_take(kind, view, beyond, half)

    def plane_finish(kind, view):
        for x in range(groups):
            for y in range(halves):
                source = index_of(at(x, y, 1 - core))
                for half in range(2):
                    landed(view(source, half), plane_recv.at[kind, source, half])

    def plane_sent(kind, view):
        for copies in plane_copies(kind, view):
            for one in copies:
                one.wait_send()
        for half in range(2):
            for x, y in near + beside + beyond:
                for one in pass_copies(kind, view, x, y, half)[1]:
                    one.wait_send()

    def tall(ref, size):
        return lambda index, half: ref.at[place(2 * index + half, size // 2)]

    def strip(index, half):
        return weights_columns.at[:, place(2 * index + half, part_rows)]

    acts_kind, projected_kind, products_kind, first_kind, strip_kind = 0, 1, 2, 3, 4

    loads[2].wait()
    acts_columns[place(row, rows)] = acts[:, place(me, width)]
    plane_start(acts_kind, tall(acts_columns, rows))

    def acts_swap(step):
        target = (row + step) % members
        return remote(
            acts.at[:, place(target, block)],
            acts_rows.at[place(row, rows)],
            swap_send.at[0, step],
            swap_recv.at[0, row],
            member_id(target),
        )

    acts_rows[place(row, rows)] = acts[:, place(row, block)]
    loads[0].wait()

    def project(index, _):
        where = place(index, tile)
        value = product(acts[...], panel[:, where])
        projected[place(row, rows), where] = value.astype(HALF)
        cubes[:, where] = (value * value * value * (1.0 / tokens)).astype(HALF)
        return 0

    lax.fori_loop(0, width // tile, project, 0)
    plane_relay(acts_kind, tall(acts_columns, rows))
    for step in range(1, members):
        acts_swap(step).start()

    def piece(ref, column, part):
        return ref.at[place(column, width), place(part, part_rows)]

    def line_copy(part, column, right, source):
        target = from_left if right else from_right
        way = 0 if right else 1
        return remote(
            piece(source, column, part),
            piece(target, column, part),
            line_send.at[part, column, way],
            line_recv.at[part, column, way],
            (dp, section, me + 1 if right else me - 1),
        )

    def add_into(target, column, part):
        lanes = place(part, part_rows)

        def one(index, _):
            where = place(column * (width // tile) + index, tile)
            target[where, lanes] = (
                target[where, lanes].astype(jnp.float32) + partial[where, lanes].astype(jnp.float32)
            ).astype(HALF)
            return 0

        lax.fori_loop(0, width // tile, one, 0)

    def first_sends(part, steps):
        for step in steps:
            right, left = columns - 1 - step, step
            pl.when(me == 0)(lambda: line_copy(part, right, True, partial).start())
            pl.when(me == columns - 1)(lambda: line_copy(part, left, False, partial).start())

    def relay_right(part, step):
        column = columns - 1 - step

        @pl.when((me > 0) & (me < column))
        def _():
            landed(piece(from_left, column, part), line_recv.at[part, column, 0])
            add_into(from_left, column, part)
            line_copy(part, column, True, from_left).start()

    def relay_left(part, step):
        column = step

        @pl.when((me < columns - 1) & (me > column))
        def _():
            landed(piece(from_right, column, part), line_recv.at[part, column, 1])
            add_into(from_right, column, part)
            line_copy(part, column, False, from_right).start()

    def relay(part, step):
        pl.when(me < columns // 2)(lambda: relay_right(part, step))
        relay_left(part, step)
        pl.when(me >= columns // 2)(lambda: relay_right(part, step))

    def line_sent(part):
        for column in range(columns):
            pl.when(me < column)(lambda: line_copy(part, column, True, partial).wait_send())
            pl.when(me > column)(lambda: line_copy(part, column, False, partial).wait_send())

    def settle(part):
        lanes = place(part, part_rows)
        pl.when(me > 0)(lambda: landed(piece(from_left, me, part), line_recv.at[part, me, 0]))
        pl.when(me < columns - 1)(lambda: landed(piece(from_right, me, part), line_recv.at[part, me, 1]))
        left = jnp.where(me > 0, 1.0, 0.0)
        right = jnp.where(me < columns - 1, 1.0, 0.0)

        def one(index, _):
            where = place(me * (width // tile) + index, tile)
            value = partial[where, lanes].astype(jnp.float32)
            value = value + jnp.where(left > 0.5, from_left[where, lanes].astype(jnp.float32), 0.0)
            value = value + jnp.where(right > 0.5, from_right[where, lanes].astype(jnp.float32), 0.0)
            final = value.astype(HALF)
            weights[where, lanes] = final
            weights_columns[place(index, tile), place(row * parts + part, part_rows)] = final
            return 0

        lax.fori_loop(0, width // tile, one, 0)

    def spread_copy(part, column, right):
        view = piece(weights, column, part)
        return remote(
            view,
            view,
            spread_send.at[part, column, 0 if right else 1],
            spread_recv.at[part, column],
            (dp, section, me + 1 if right else me - 1),
        )

    def weights_swap(part, target):
        return remote(
            weights.at[place(target, block), place(part, part_rows)],
            weights_rows.at[:, place(row * parts + part, part_rows)],
            swap_send.at[1 + part, target],
            swap_recv.at[1 + part, row],
            member_id(target),
        )

    def hand_out(part, column):
        for index in range(per_column):
            target = column * per_column + index
            pl.when(target != row)(lambda: weights_swap(part, target).start())

            @pl.when(target == row)
            def _():
                weights_rows[:, place(row * parts + part, part_rows)] = weights[
                    place(row, block), place(part, part_rows)
                ]

    def offer(part):
        pl.when(me + 1 < columns)(lambda: spread_copy(part, me, True).start())
        pl.when(me > 0)(lambda: spread_copy(part, me, False).start())
        plane_start(strip_kind, strip, (part,))
        hand_out(part, me)

    def spread(part, step):
        @pl.when(me >= step)
        def _():
            landed(piece(weights, me - step, part), spread_recv.at[part, me - step])
            pl.when(me + 1 < columns)(lambda: spread_copy(part, me - step, True).start())
            hand_out(part, me - step)

        @pl.when(me + step < columns)
        def _():
            landed(piece(weights, me + step, part), spread_recv.at[part, me + step])
            pl.when(me > 0)(lambda: spread_copy(part, me + step, False).start())
            hand_out(part, me + step)

    def spread_sent(part):
        for column in range(columns):
            pl.when((column <= me) & (me + 1 < columns))(lambda: spread_copy(part, column, True).wait_send())
            pl.when((column >= me) & (me > 0))(lambda: spread_copy(part, column, False).wait_send())

    steps = range(columns - 1)

    def weigh(index, _):
        where = place(jnp.where(me < columns // 2, columns - 1 - index, index), width)
        partial[where] = product(panel[where], cubes[...], 1, 1).astype(HALF)
        return 0

    for step in steps:
        weigh(step, 0)
        first_sends(0, [step])
    weigh(columns - 1, 0)
    first_sends(1, steps[:1])
    for step in steps:
        relay(0, step)
    settle(0)
    offer(0)
    first_sends(1, steps[1:])
    for step in steps:
        relay(1, step)
        spread(0, step + 1)
    settle(1)
    offer(1)
    plane_take(strip_kind, strip, near, 0)
    plane_rest(acts_kind, tall(acts_columns, rows))
    for other in range(1, members):
        source = (row + other) % members
        landed(acts_rows.at[place(source, rows)], swap_recv.at[0, source])

    def turn(index, _):
        acts_turned[:, place(index, rows)] = acts_rows[place(index, rows)].T
        return 0

    for step in steps:
        spread(1, step + 1)
        if step == 0:
            plane_take(strip_kind, strip, beside, 1)
    lax.fori_loop(0, members, turn, 0)

    def apply(index, _):
        where = place(index, width)
        total[...] += product(weights[where], panel[where], 0, 0)
        return 0

    total[...] = jnp.zeros_like(total)
    lax.fori_loop(0, columns, apply, 0)
    products[place(row, rows)] = total[...].astype(HALF)
    plane_start(products_kind, tall(products, rows))
    plane_start(projected_kind, tall(projected, rows))

    plane_rest(strip_kind, strip)
    plane_finish(acts_kind, tall(acts_columns, rows))
    for part in range(parts):
        for other in range(1, members):
            source = (row + other) % members
            landed(weights_rows.at[:, place(source * parts + part, part_rows)], swap_recv.at[1 + part, source])
    plane_finish(strip_kind, strip)

    def build(index, squares):
        where = place(index, tile)
        value = product(acts_turned[...], weights_columns[where], 1, 1) - product(
            weights_rows[...], acts_columns[:, where]
        )
        skew[me, :, where] = value.astype(HALF)
        return squares + jnp.sum(value * value)

    squares = lax.fori_loop(0, width // tile, build, jnp.float32(0.0))

    def skew_copy(column, right):
        view = skew.at[column]
        return remote(
            view,
            view,
            skew_send.at[column, 0 if right else 1],
            skew_recv.at[column],
            (dp, section, me + 1 if right else me - 1),
        )

    pl.when(me + 1 < columns)(lambda: skew_copy(me, True).start())
    pl.when(me > 0)(lambda: skew_copy(me, False).start())

    def skew_pass(step):
        @pl.when(me >= step)
        def _():
            landed(skew.at[me - step], skew_recv.at[me - step])
            pl.when(me + 1 < columns)(lambda: skew_copy(me - step, True).start())

        @pl.when(me + step < columns)
        def _():
            landed(skew.at[me + step], skew_recv.at[me + step])
            pl.when(me > 0)(lambda: skew_copy(me + step, False).start())

    def skew_sent():
        for column in range(columns):
            pl.when((column <= me) & (me + 1 < columns))(lambda: skew_copy(column, True).wait_send())
            pl.when((column >= me) & (me > 0))(lambda: skew_copy(column, False).wait_send())

    norms_line[me] = jnp.full(norms_line.shape[1:], squares, jnp.float32)

    def norm_line_copy(step):
        other = (me + step) % columns
        return remote(
            norms_line.at[me], norms_line.at[me], norm_send.at[0, step], norm_recv.at[0, me], (dp, section, other)
        )

    def norm_plane_copy(step):
        return remote(
            norms_plane.at[row],
            norms_plane.at[row],
            norm_send.at[1, step],
            norm_recv.at[1, row],
            member_id((row + step) % members),
        )

    for step in range(1, columns):
        norm_line_copy(step).start()

    plane_relay(products_kind, tall(products, rows))
    plane_relay(projected_kind, tall(projected, rows))
    for step in range(1, columns):
        other = (me + step) % columns
        landed(norms_line.at[other], norm_recv.at[0, other])
    norms_plane[row] = jnp.sum(norms_line[...], axis=0)
    for step in range(1, members):
        norm_plane_copy(step).start()
    skew_pass(1)
    plane_rest(products_kind, tall(products, rows))
    plane_rest(projected_kind, tall(projected, rows))
    plane_finish(products_kind, tall(products, rows))
    plane_finish(projected_kind, tall(projected, rows))

    for half in range(2):
        lines = slice(half * (block // 2), (half + 1) * (block // 2))

        def multiply(index, _):
            where = place(index, tile)
            value = product(acts_turned[lines], products[:, where]) - product(weights_rows[lines], projected[:, where])
            out[lines, where] = value
            first[place(2 * row + half, block // 2), where] = value.astype(HALF)
            return 0

        lax.fori_loop(0, width // tile, multiply, 0)
        plane_start(first_kind, tall(first, block), (half,))
    for step in range(2, columns - 1):
        skew_pass(step)
    plane_relay(first_kind, tall(first, block))
    plane_rest(first_kind, tall(first, block))
    skew_pass(columns - 1)
    loads[1].wait()
    for step in range(1, members):
        other = (row + step) % members
        landed(norms_plane.at[other], norm_recv.at[1, other])
    plane_finish(first_kind, tall(first, block))

    mean_square = jnp.sum(norms_plane[...], axis=0)[0:1, 0:1] / (full * full)
    scale = 0.5 * lax.rsqrt(full * (mean_square + 1e-06))
    root = math.sqrt(full)

    def finish(index, _):
        where = place(index, tile)
        value = jnp.zeros((block, tile), jnp.float32)
        for column in range(columns):
            value = value + product(skew[column], first[column * width : (column + 1) * width, where])
        out[:, where] = own[:, where] - (root * scale) * out[:, where] + (0.5 * root * scale * scale) * value
        return 0

    lax.fori_loop(0, width // tile, finish, 0)

    for part in range(parts):
        line_sent(part)
        spread_sent(part)
        for target in range(members):
            pl.when(target != row)(lambda: weights_swap(part, target).wait_send())
    for step in range(1, members):
        acts_swap(step).wait_send()
        norm_plane_copy(step).wait_send()
    for step in range(1, columns):
        norm_line_copy(step).wait_send()
    skew_sent()
    plane_sent(strip_kind, strip)
    plane_sent(acts_kind, tall(acts_columns, rows))
    plane_sent(projected_kind, tall(projected, rows))
    plane_sent(products_kind, tall(products, rows))
    plane_sent(first_kind, tall(first, block))


def run_update(acts, panel, rotation, tokens):
    rows, full = acts.shape
    block, width = rotation.shape
    columns = lax.axis_size("tensor")
    members = lax.axis_size("dp") * lax.axis_size("layer")
    groups, halves = lax.axis_size("dp"), lax.axis_size("layer") // 2
    parts = 2
    kinds = 5
    held = members * rows
    dma = pltpu.SemaphoreType.DMA
    return pl.pallas_call(
        functools.partial(update_kernel, tokens),
        out_shape=jax.ShapeDtypeStruct((block, width), jnp.float32),
        in_specs=[pl.BlockSpec(memory_space=pl.ANY)] * 3,
        out_specs=pl.BlockSpec(memory_space=pltpu.VMEM),
        scratch_shapes=[
            pltpu.VMEM((rows, full), HALF),
            pltpu.VMEM((full, width), HALF),
            pltpu.VMEM((block, width), jnp.float32),
            pltpu.VMEM((rows, width), HALF),
            pltpu.VMEM((full, rows), HALF),
            pltpu.VMEM((full, rows), HALF),
            pltpu.VMEM((full, rows), HALF),
            pltpu.VMEM((full, rows), HALF),
            pltpu.VMEM((held, width), HALF),
            pltpu.VMEM((held, block), HALF),
            pltpu.VMEM((block, held), HALF),
            pltpu.VMEM((width, held), HALF),
            pltpu.VMEM((block, held), HALF),
            pltpu.VMEM((held, width), HALF),
            pltpu.VMEM((held, width), HALF),
            pltpu.VMEM((rows, width), jnp.float32),
            pltpu.VMEM((columns, block, width), HALF),
            pltpu.VMEM((full, width), HALF),
            pltpu.VMEM((columns, 8, 128), jnp.float32),
            pltpu.VMEM((members, 8, 128), jnp.float32),
            dma((parts, columns, 2)),
            dma((parts, columns, 2)),
            dma((parts, columns, 2)),
            dma((parts, columns)),
            dma((kinds, 2, groups + halves)),
            dma((kinds, 2, groups * halves)),
            dma((kinds, 2, groups, halves)),
            dma((kinds, members, 2)),
            dma((1 + parts, members)),
            dma((1 + parts, members)),
            dma((columns, 2)),
            dma((columns,)),
            dma((2, max(members, columns))),
            dma((2, max(members, columns))),
            dma((3,)),
        ],
        compiler_params=pltpu.CompilerParams(
            collective_id=1, has_side_effects=True, vmem_limit_bytes=62 * 1024 * 1024
        ),
        cost_estimate=pl.CostEstimate(
            flops=2 * full * full * full // 4, bytes_accessed=full * width * 8, transcendentals=0
        ),
    )(acts, panel, rotation)


def shards(embeddings, layer_weight, rotation):
    full = layer_weight.shape[1]
    head = (rotation / math.sqrt(full)).astype(HALF)
    panel = lax.all_gather(head, ROWS, axis=0, tiled=True)
    acts = run_layers(embeddings, layer_weight)
    return run_update(acts, panel, rotation, embeddings.shape[0] * lax.axis_size("dp"))


def solution(mesh):
    return jax.shard_map(
        shards,
        mesh=mesh,
        in_specs=(P("dp", "tensor"), P("layer", None, "tensor"), P(("dp", "layer"), "tensor")),
        out_specs=P(("dp", "layer"), "tensor"),
        check_vma=False,
    )
```

```python
import functools
import math

import jax
import jax.numpy as jnp
from jax import lax
from jax.experimental import pallas as pl
from jax.experimental.pallas import tpu as pltpu
from jax.sharding import PartitionSpec as P

ROWS = ("dp", "layer")
EVERY = ("dp", "layer", "tensor")
HALF = jnp.bfloat16
CHUNKS = 4
LAG = 1
REACH = 2
UPPERS = 1
MESH = pl.DeviceIdType.MESH


def product(left, right, left_dim=1, right_dim=0):
    dims = (((left_dim,), (right_dim,)), ((), ()))
    return lax.dot_general(left, right, dims, preferred_element_type=jnp.float32)


def layers_kernel(
    chunks,
    embeddings,
    weight_hbm,
    records,
    hidden,
    outbox,
    weight,
    update,
    squares,
    send_sem,
    pass_sem,
    recv_sem,
    weight_sem,
):
    dp, section, me = (lax.axis_index(name) for name in EVERY)
    sections, columns = lax.axis_size("layer"), lax.axis_size("tensor")
    levels = weight_hbm.shape[0]
    width = embeddings.shape[1]
    rows = embeddings.shape[0] // chunks
    full = columns * width
    distances = []
    for base in range(0, columns - 1, REACH):
        group = [d for d in range(base + 1, base + REACH + 1) if d < columns]
        distances += group[-1:] + group[:-1] if base + REACH + 1 < columns else group

    loads = [
        pltpu.make_async_copy(weight_hbm.at[level], weight.at[level], weight_sem.at[level])
        for level in range(levels)
    ]
    loads[0].start()

    barrier = pltpu.get_barrier_semaphore()

    def greet(row, column):
        pl.semaphore_signal(barrier, inc=1, device_id=(dp, row, column), device_id_type=MESH)

    for column in range(columns):
        pl.when(column != me)(lambda column=column: greet(section, column))
        pl.when(section > 0)(lambda column=column: greet(section - 1, column))
        pl.when(section + 1 < sections)(lambda column=column: greet(section + 1, column))
    edges = jnp.where(section > 0, 1, 0) + jnp.where(section + 1 < sections, 1, 0)
    pl.semaphore_wait(barrier, columns - 1 + columns * edges)
    for load in loads[1:]:
        load.start()

    def remote(source, target, send, recv, row, column):
        return pltpu.make_async_remote_copy(
            src_ref=source,
            dst_ref=target,
            send_sem=send,
            recv_sem=recv,
            device_id=(dp, row, column),
            device_id_type=MESH,
        )

    def own_copy(stage, chunk, offset):
        level, row = (stage, section) if stage < levels else (0, section + 1)
        source = hidden.at[stage, chunk, me] if stage < levels else outbox.at[chunk]
        return remote(
            source,
            hidden.at[level, chunk, me],
            send_sem.at[stage, chunk, offset + REACH],
            recv_sem.at[level, chunk, me],
            row,
            me + offset,
        )

    def own_copies(stage, chunk, action):
        for reach in range(REACH, -1, -1):
            for offset in (reach, -reach) if reach else (0,):
                wanted = (me + offset >= 0) & (me + offset < columns)
                if stage == levels:
                    wanted = wanted & (section + 1 < sections)
                elif offset == 0:
                    continue
                elif stage == 0:
                    wanted = wanted & (section == 0)
                pl.when(wanted)(lambda offset=offset: action(own_copy(stage, chunk, offset)))

    def pass_copy(level, chunk, source, offset):
        view = hidden.at[level, chunk, source]
        return remote(
            view,
            view,
            pass_sem.at[level, chunk, source, abs(offset) - 1],
            recv_sem.at[level, chunk, source],
            section,
            me + offset,
        )

    def passes(level, chunk, distance, way, action):
        if distance % REACH or distance + 1 >= columns:
            return
        source = me - way * distance
        for reach in range(REACH, 0, -1):
            target = me + way * reach
            pl.when((target >= 0) & (target < columns))(
                lambda reach=reach: action(pass_copy(level, chunk, source, way * reach))
            )

    def arrive(level, chunk, source):
        view = hidden.at[level, chunk, source]
        remote(view, view, recv_sem.at[level, chunk, source], recv_sem.at[level, chunk, source], section, me).wait_recv()

    def gather_in(level, chunk, source, first=False):
        value = hidden[level, chunk, source]
        wide = value.astype(jnp.float32)
        square = jnp.sum(wide * wide, axis=-1, keepdims=True)
        part = product(value, weight[level, pl.ds(pl.multiple_of(source * width, width), width), :])
        squares[...] = square if first else squares[...] + square
        update[...] = part if first else update[...] + part

    def step(level, chunk):
        if level == 0:
            pl.when(section > 0)(lambda: arrive(level, chunk, me))
        gather_in(level, chunk, me, True)
        for distance in distances:
            for way in (1, -1):
                source = me - way * distance

                @pl.when((source >= 0) & (source < columns))
                def _():
                    arrive(level, chunk, source)
                    passes(level, chunk, distance, way, lambda one: one.start())
                    gather_in(level, chunk, source)

        inverse = lax.rsqrt(squares[...] / full + 1e-05)
        fresh = (hidden[level, chunk, me].astype(jnp.float32) + inverse * update[...]).astype(HALF)
        if level + 1 < levels:
            hidden[level + 1, chunk, me] = fresh
        else:
            outbox[chunk] = fresh
        own_copies(level + 1, chunk, lambda one: one.start())
        for column in range(columns):
            wide = hidden[level, chunk, column].astype(jnp.float32)
            records[level, chunk, :, column * width : (column + 1) * width] = (wide * inverse).astype(HALF)

    @pl.when(section == 0)
    def _():
        for chunk in range(chunks):
            hidden[0, chunk, me] = embeddings[chunk * rows : (chunk + 1) * rows, :]

    for chunk in range(chunks):
        own_copies(0, chunk, lambda one: one.start())

    def turn(index, _):
        for level in range(levels):
            chunk = index - level * LAG

            @pl.when((chunk >= 0) & (chunk < chunks))
            def _():
                pl.when(chunk == 0)(lambda: loads[level].wait())
                step(level, chunk)

        return 0

    lax.fori_loop(0, chunks + (levels - 1) * LAG, turn, 0)

    for chunk in range(chunks):
        for stage in range(levels + 1):
            own_copies(stage, chunk, lambda one: one.wait_send())
        for level in range(levels):
            for distance in distances:
                for way in (1, -1):
                    source = me - way * distance
                    pl.when((source >= 0) & (source < columns))(
                        lambda distance=distance, way=way: passes(
                            level, chunk, distance, way, lambda one: one.wait_send()
                        )
                    )


def run_layers(embeddings, layer_weight):
    levels, full, width = layer_weight.shape
    tokens = embeddings.shape[0]
    columns = lax.axis_size("tensor")
    rows = tokens // CHUNKS
    dma = pltpu.SemaphoreType.DMA
    records = pl.pallas_call(
        functools.partial(layers_kernel, CHUNKS),
        out_shape=jax.ShapeDtypeStruct((levels, CHUNKS, rows, full), HALF),
        in_specs=[pl.BlockSpec(memory_space=pltpu.VMEM), pl.BlockSpec(memory_space=pl.ANY)],
        out_specs=pl.BlockSpec(memory_space=pltpu.VMEM),
        scratch_shapes=[
            pltpu.VMEM((levels, CHUNKS, columns, rows, width), HALF),
            pltpu.VMEM((CHUNKS, rows, width), HALF),
            pltpu.VMEM((levels, full, width), HALF),
            pltpu.VMEM((rows, width), jnp.float32),
            pltpu.VMEM((rows, 1), jnp.float32),
            dma((levels + 1, CHUNKS, 2 * REACH + 1)),
            dma((levels, CHUNKS, columns, REACH)),
            dma((levels, CHUNKS, columns)),
            dma((levels,)),
        ],
        compiler_params=pltpu.CompilerParams(
            collective_id=0, has_side_effects=True, vmem_limit_bytes=40 * 1024 * 1024
        ),
        cost_estimate=pl.CostEstimate(
            flops=2 * tokens * full * width * levels * 40,
            bytes_accessed=layer_weight.size * 2 * 20,
            transcendentals=0,
        ),
    )(embeddings, layer_weight)
    return records.reshape(levels * tokens, full)


def update_kernel(
    tokens,
    acts_hbm,
    panel_hbm,
    own_hbm,
    out,
    acts,
    panel,
    own,
    cubes,
    partial,
    from_left,
    from_right,
    weights,
    acts_columns,
    acts_rows,
    acts_turned,
    weights_columns,
    weights_rows,
    projected,
    products,
    total,
    skew,
    first,
    norms_line,
    norms_plane,
    line_send,
    line_recv,
    spread_send,
    spread_recv,
    plane_send,
    plane_pass,
    plane_cross,
    plane_recv,
    swap_send,
    swap_recv,
    skew_send,
    skew_recv,
    norm_send,
    norm_recv,
    load_sem,
):
    dp, section, me = (lax.axis_index(name) for name in EVERY)
    groups, sections, columns = (lax.axis_size(name) for name in EVERY)
    loads = [
        pltpu.make_async_copy(panel_hbm, panel, load_sem.at[0]),
        pltpu.make_async_copy(own_hbm, own, load_sem.at[1]),
        pltpu.make_async_copy(acts_hbm, acts, load_sem.at[2]),
    ]
    loads[2].start()
    loads[0].start()
    rows, full = acts_hbm.shape
    block, width = own_hbm.shape
    members = groups * sections
    halves = sections // 2
    core = section % 2
    side = section // 2
    row = dp * sections + section
    tile = min(256, width)
    parts = 2
    part_rows = rows // parts
    per_column = width // block

    def place(index, size):
        return pl.ds(pl.multiple_of(index * size, size), size)

    def member_id(index):
        return (index // sections, index % sections, me)

    def at(across, along, which):
        return (dp + across) % groups, ((side + along) % halves) * 2 + which

    def index_of(spot):
        return spot[0] * sections + spot[1]

    def remote(source, target, send, recv, device):
        return pltpu.make_async_remote_copy(
            src_ref=source, dst_ref=target, send_sem=send, recv_sem=recv, device_id=device, device_id_type=MESH
        )

    def landed(target, recv):
        remote(target, target, recv, recv, (dp, section, me)).wait_recv()

    barrier = pltpu.get_barrier_semaphore()
    for step in range(1, members):
        pl.semaphore_signal(barrier, inc=1, device_id=member_id((row + step) % members), device_id_type=MESH)
    for step in range(1, columns):
        pl.semaphore_signal(barrier, inc=1, device_id=(dp, section, (me + step) % columns), device_id_type=MESH)
    pl.semaphore_wait(barrier, members - 1 + columns - 1)

    def send_to(view, source, half, spot, send, kind):
        piece = view(source, half)
        return remote(piece, piece, send, plane_recv.at[kind, source, half], (spot[0], spot[1], me))

    def plane_copies(kind, view, which=(0, 1)):
        def across(half):
            return [
                send_to(view, row, half, at(x, 0, core), plane_send.at[kind, half, x], kind) for x in range(1, groups)
            ]

        def along(half):
            return [
                send_to(view, row, half, at(0, y, core), plane_send.at[kind, half, groups + y], kind)
                for y in range(1, halves)
            ]

        def other(half):
            return [send_to(view, row, half, at(0, 0, 1 - core), plane_send.at[kind, half, 0], kind)]

        return [
            along(half) + across(half) + other(half) if half else across(half) + along(half) + other(half)
            for half in which
        ]

    def pass_copies(kind, view, x, y, half):
        source = index_of(at(x, y, core))
        copies = []
        if half == 0 and y == 0:
            copies += [
                send_to(view, source, half, at(0, z, core), plane_cross.at[kind, half, x, z], kind)
                for z in range(1, halves)
            ]
        if half == 1 and x == 0:
            copies += [
                send_to(view, source, half, at(z, 0, core), plane_cross.at[kind, half, z, y], kind)
                for z in range(1, groups)
            ]
        copies.append(send_to(view, source, half, at(0, 0, 1 - core), plane_pass.at[kind, half, x * halves + y], kind))
        return source, copies

    def plane_start(kind, view, which=(0, 1)):
        copies = plane_copies(kind, view, which)
        most = max(len(one) for one in copies)
        for spot in range(most):
            for one in copies:
                if spot < len(one):
                    one[spot].start()

    near = [(x, 0) for x in range(1, groups)]
    beside = [(0, y) for y in range(1, halves)]
    beyond = [(x, y) for x in range(1, groups) for y in range(1, halves)]

    def plane_take(kind, view, spots, half):
        for x, y in spots:
            source, copies = pass_copies(kind, view, x, y, half)
            landed(view(source, half), plane_recv.at[kind, source, half])
            for one in copies:
                one.start()

    def plane_relay(kind, view):
        plane_take(kind, view, near, 0)
        plane_take(kind, view, beside, 1)

    def plane_rest(kind, view):
        plane_take(kind, view, near, 1)
        plane_take(kind, view, beside, 0)
        for half in range(2):
            plane_take(kind, view, beyond, half)

    def plane_finish(kind, view):
        for x in range(groups):
            for y in range(halves):
                source = index_of(at(x, y, 1 - core))
                for half in range(2):
                    landed(view(source, half), plane_recv.at[kind, source, half])

    def plane_sent(kind, view):
        for copies in plane_copies(kind, view):
            for one in copies:
                one.wait_send()
        for half in range(2):
            for x, y in near + beside + beyond:
                for one in pass_copies(kind, view, x, y, half)[1]:
                    one.wait_send()

    def tall(ref, size):
        return lambda index, half: ref.at[place(2 * index + half, size // 2)]

    def strip(index, half):
        return weights_columns.at[:, place(2 * index + half, part_rows)]

    acts_kind, projected_kind, products_kind, first_kind, strip_kind = 0, 1, 2, 3, 4

    loads[2].wait()
    acts_columns[place(row, rows)] = acts[:, place(me, width)]
    plane_start(acts_kind, tall(acts_columns, rows))

    def acts_swap(step):
        target = (row + step) % members
        return remote(
            acts.at[:, place(target, block)],
            acts_rows.at[place(row, rows)],
            swap_send.at[0, step],
            swap_recv.at[0, row],
            member_id(target),
        )

    acts_rows[place(row, rows)] = acts[:, place(row, block)]
    loads[0].wait()
    loads[1].start()

    def project(index, _):
        where = place(index, tile)
        value = product(acts[...], panel[:, where])
        projected[place(row, rows), where] = value.astype(HALF)
        cubes[:, where] = (value * value * value * (1.0 / tokens)).astype(HALF)
        return 0

    lax.fori_loop(0, width // tile, project, 0)
    plane_relay(acts_kind, tall(acts_columns, rows))
    for step in range(1, members):
        acts_swap(step).start()

    def piece(ref, column, part):
        return ref.at[place(column, width), place(part, part_rows)]

    def line_copy(part, column, right, source):
        target = from_left if right else from_right
        way = 0 if right else 1
        return remote(
            piece(source, column, part),
            piece(target, column, part),
            line_send.at[part, column, way],
            line_recv.at[part, column, way],
            (dp, section, me + 1 if right else me - 1),
        )

    def add_into(target, column, part):
        lanes = place(part, part_rows)

        def one(index, _):
            where = place(column * (width // tile) + index, tile)
            target[where, lanes] = (
                target[where, lanes].astype(jnp.float32) + partial[where, lanes].astype(jnp.float32)
            ).astype(HALF)
            return 0

        lax.fori_loop(0, width // tile, one, 0)

    def first_sends(part, steps):
        for step in steps:
            right, left = columns - 1 - step, step
            pl.when(me == 0)(lambda: line_copy(part, right, True, partial).start())
            pl.when(me == columns - 1)(lambda: line_copy(part, left, False, partial).start())

    def relay_right(part, step):
        column = columns - 1 - step

        @pl.when((me > 0) & (me < column))
        def _():
            landed(piece(from_left, column, part), line_recv.at[part, column, 0])
            add_into(from_left, column, part)
            line_copy(part, column, True, from_left).start()

    def relay_left(part, step):
        column = step

        @pl.when((me < columns - 1) & (me > column))
        def _():
            landed(piece(from_right, column, part), line_recv.at[part, column, 1])
            add_into(from_right, column, part)
            line_copy(part, column, False, from_right).start()

    def relay(part, step):
        pl.when(me < columns // 2)(lambda: relay_right(part, step))
        relay_left(part, step)
        pl.when(me >= columns // 2)(lambda: relay_right(part, step))

    def line_sent(part):
        for column in range(columns):
            pl.when(me < column)(lambda: line_copy(part, column, True, partial).wait_send())
            pl.when(me > column)(lambda: line_copy(part, column, False, partial).wait_send())

    def settle(part):
        lanes = place(part, part_rows)
        pl.when(me > 0)(lambda: landed(piece(from_left, me, part), line_recv.at[part, me, 0]))
        pl.when(me < columns - 1)(lambda: landed(piece(from_right, me, part), line_recv.at[part, me, 1]))
        left = jnp.where(me > 0, 1.0, 0.0)
        right = jnp.where(me < columns - 1, 1.0, 0.0)

        def one(index, _):
            where = place(me * (width // tile) + index, tile)
            value = partial[where, lanes].astype(jnp.float32)
            value = value + jnp.where(left > 0.5, from_left[where, lanes].astype(jnp.float32), 0.0)
            value = value + jnp.where(right > 0.5, from_right[where, lanes].astype(jnp.float32), 0.0)
            final = value.astype(HALF)
            weights[where, lanes] = final
            weights_columns[place(index, tile), place(row * parts + part, part_rows)] = final
            return 0

        lax.fori_loop(0, width // tile, one, 0)

    def spread_copy(part, column, right):
        view = piece(weights, column, part)
        return remote(
            view,
            view,
            spread_send.at[part, column, 0 if right else 1],
            spread_recv.at[part, column],
            (dp, section, me + 1 if right else me - 1),
        )

    def weights_swap(part, target):
        return remote(
            weights.at[place(target, block), place(part, part_rows)],
            weights_rows.at[:, place(row * parts + part, part_rows)],
            swap_send.at[1 + part, target],
            swap_recv.at[1 + part, row],
            member_id(target),
        )

    def hand_out(part, column):
        for index in range(per_column):
            target = column * per_column + index
            pl.when(target != row)(lambda: weights_swap(part, target).start())

            @pl.when(target == row)
            def _():
                weights_rows[:, place(row * parts + part, part_rows)] = weights[
                    place(row, block), place(part, part_rows)
                ]

    def offer(part):
        pl.when(me + 1 < columns)(lambda: spread_copy(part, me, True).start())
        pl.when(me > 0)(lambda: spread_copy(part, me, False).start())
        plane_start(strip_kind, strip, (part,))
        hand_out(part, me)

    def spread(part, step):
        @pl.when(me >= step)
        def _():
            landed(piece(weights, me - step, part), spread_recv.at[part, me - step])
            pl.when(me + 1 < columns)(lambda: spread_copy(part, me - step, True).start())
            hand_out(part, me - step)

        @pl.when(me + step < columns)
        def _():
            landed(piece(weights, me + step, part), spread_recv.at[part, me + step])
            pl.when(me > 0)(lambda: spread_copy(part, me + step, False).start())
            hand_out(part, me + step)

    def spread_sent(part):
        for column in range(columns):
            pl.when((column <= me) & (me + 1 < columns))(lambda: spread_copy(part, column, True).wait_send())
            pl.when((column >= me) & (me > 0))(lambda: spread_copy(part, column, False).wait_send())

    steps = range(columns - 1)

    def weigh(index, _):
        where = place(jnp.where(me < columns // 2, columns - 1 - index, index), width)
        partial[where] = product(panel[where], cubes[...], 1, 1).astype(HALF)
        return 0

    for step in steps:
        weigh(step, 0)
        first_sends(0, [step])
    weigh(columns - 1, 0)
    first_sends(1, steps[:1])
    for step in steps:
        relay(0, step)
    settle(0)
    offer(0)
    first_sends(1, steps[1:])
    for step in steps:
        relay(1, step)
        spread(0, step + 1)
    settle(1)
    offer(1)
    plane_take(strip_kind, strip, near, 0)
    plane_rest(acts_kind, tall(acts_columns, rows))
    for other in range(1, members):
        source = (row + other) % members
        landed(acts_rows.at[place(source, rows)], swap_recv.at[0, source])

    def turn(index, _):
        acts_turned[:, place(index, rows)] = acts_rows[place(index, rows)].T
        return 0

    for step in steps:
        spread(1, step + 1)
        if step == 0:
            plane_take(strip_kind, strip, beside, 1)
    lax.fori_loop(0, members, turn, 0)

    def apply(index, _):
        where = place(index, width)
        total[...] += product(weights[where], panel[where], 0, 0)
        return 0

    total[...] = jnp.zeros_like(total)
    lax.fori_loop(0, columns, apply, 0)
    products[place(row, rows)] = total[...].astype(HALF)
    plane_start(products_kind, tall(products, rows))
    plane_start(projected_kind, tall(projected, rows))

    plane_rest(strip_kind, strip)
    plane_finish(acts_kind, tall(acts_columns, rows))
    for part in range(parts):
        for other in range(1, members):
            source = (row + other) % members
            landed(weights_rows.at[:, place(source * parts + part, part_rows)], swap_recv.at[1 + part, source])
    plane_finish(strip_kind, strip)

    def build(index, squares):
        where = place(index, tile)
        value = product(acts_turned[...], weights_columns[where], 1, 1) - product(
            weights_rows[...], acts_columns[:, where]
        )
        skew[me, :, where] = value.astype(HALF)
        return squares + jnp.sum(value * value)

    squares = lax.fori_loop(0, width // tile, build, jnp.float32(0.0))

    def skew_copy(column, right):
        view = skew.at[column]
        return remote(
            view,
            view,
            skew_send.at[column, 0 if right else 1],
            skew_recv.at[column],
            (dp, section, me + 1 if right else me - 1),
        )

    pl.when(me + 1 < columns)(lambda: skew_copy(me, True).start())
    pl.when(me > 0)(lambda: skew_copy(me, False).start())

    def skew_pass(step):
        @pl.when(me >= step)
        def _():
            landed(skew.at[me - step], skew_recv.at[me - step])
            pl.when(me + 1 < columns)(lambda: skew_copy(me - step, True).start())

        @pl.when(me + step < columns)
        def _():
            landed(skew.at[me + step], skew_recv.at[me + step])
            pl.when(me > 0)(lambda: skew_copy(me + step, False).start())

    def skew_sent():
        for column in range(columns):
            pl.when((column <= me) & (me + 1 < columns))(lambda: skew_copy(column, True).wait_send())
            pl.when((column >= me) & (me > 0))(lambda: skew_copy(column, False).wait_send())

    norms_line[me] = jnp.full(norms_line.shape[1:], squares, jnp.float32)

    def norm_line_copy(step):
        other = (me + step) % columns
        return remote(
            norms_line.at[me], norms_line.at[me], norm_send.at[0, step], norm_recv.at[0, me], (dp, section, other)
        )

    def norm_plane_copy(step):
        return remote(
            norms_plane.at[row],
            norms_plane.at[row],
            norm_send.at[1, step],
            norm_recv.at[1, row],
            member_id((row + step) % members),
        )

    for step in range(1, columns):
        norm_line_copy(step).start()

    plane_relay(products_kind, tall(products, rows))
    plane_relay(projected_kind, tall(projected, rows))
    for step in range(1, columns):
        other = (me + step) % columns
        landed(norms_line.at[other], norm_recv.at[0, other])
    norms_plane[row] = jnp.sum(norms_line[...], axis=0)
    for step in range(1, members):
        norm_plane_copy(step).start()
    skew_pass(1)
    plane_rest(products_kind, tall(products, rows))
    plane_rest(projected_kind, tall(projected, rows))
    plane_finish(products_kind, tall(products, rows))
    plane_finish(projected_kind, tall(projected, rows))

    for half in range(2):
        lines = slice(half * (block // 2), (half + 1) * (block // 2))

        def multiply(index, _):
            where = place(index, tile)
            value = product(acts_turned[lines], products[:, where]) - product(weights_rows[lines], projected[:, where])
            out[lines, where] = value
            first[place(2 * row + half, block // 2), where] = value.astype(HALF)
            return 0

        lax.fori_loop(0, width // tile, multiply, 0)
        plane_start(first_kind, tall(first, block), (half,))
    for step in range(2, columns - 1):
        skew_pass(step)
    plane_relay(first_kind, tall(first, block))
    plane_rest(first_kind, tall(first, block))
    skew_pass(columns - 1)
    loads[1].wait()
    for step in range(1, members):
        other = (row + step) % members
        landed(norms_plane.at[other], norm_recv.at[1, other])
    plane_finish(first_kind, tall(first, block))

    mean_square = jnp.sum(norms_plane[...], axis=0)[0:1, 0:1] / (full * full)
    scale = 0.5 * lax.rsqrt(full * (mean_square + 1e-06))
    root = math.sqrt(full)

    def finish(index, _):
        where = place(index, tile)
        value = jnp.zeros((block, tile), jnp.float32)
        for column in range(columns):
            value = value + product(skew[column], first[column * width : (column + 1) * width, where])
        out[:, where] = own[:, where] - (root * scale) * out[:, where] + (0.5 * root * scale * scale) * value
        return 0

    lax.fori_loop(0, width // tile, finish, 0)

    for part in range(parts):
        line_sent(part)
        spread_sent(part)
        for target in range(members):
            pl.when(target != row)(lambda: weights_swap(part, target).wait_send())
    for step in range(1, members):
        acts_swap(step).wait_send()
        norm_plane_copy(step).wait_send()
    for step in range(1, columns):
        norm_line_copy(step).wait_send()
    skew_sent()
    plane_sent(strip_kind, strip)
    plane_sent(acts_kind, tall(acts_columns, rows))
    plane_sent(projected_kind, tall(projected, rows))
    plane_sent(products_kind, tall(products, rows))
    plane_sent(first_kind, tall(first, block))


def run_update(acts, panel, rotation, tokens):
    rows, full = acts.shape
    block, width = rotation.shape
    columns = lax.axis_size("tensor")
    members = lax.axis_size("dp") * lax.axis_size("layer")
    groups, halves = lax.axis_size("dp"), lax.axis_size("layer") // 2
    parts = 2
    kinds = 5
    held = members * rows
    dma = pltpu.SemaphoreType.DMA
    return pl.pallas_call(
        functools.partial(update_kernel, tokens),
        out_shape=jax.ShapeDtypeStruct((block, width), jnp.float32),
        in_specs=[pl.BlockSpec(memory_space=pl.ANY)] * 3,
        out_specs=pl.BlockSpec(memory_space=pltpu.VMEM),
        scratch_shapes=[
            pltpu.VMEM((rows, full), HALF),
            pltpu.VMEM((full, width), HALF),
            pltpu.VMEM((block, width), jnp.float32),
            pltpu.VMEM((rows, width), HALF),
            pltpu.VMEM((full, rows), HALF),
            pltpu.VMEM((full, rows), HALF),
            pltpu.VMEM((full, rows), HALF),
            pltpu.VMEM((full, rows), HALF),
            pltpu.VMEM((held, width), HALF),
            pltpu.VMEM((held, block), HALF),
            pltpu.VMEM((block, held), HALF),
            pltpu.VMEM((width, held), HALF),
            pltpu.VMEM((block, held), HALF),
            pltpu.VMEM((held, width), HALF),
            pltpu.VMEM((held, width), HALF),
            pltpu.VMEM((rows, width), jnp.float32),
            pltpu.VMEM((columns, block, width), HALF),
            pltpu.VMEM((full, width), HALF),
            pltpu.VMEM((columns, 8, 128), jnp.float32),
            pltpu.VMEM((members, 8, 128), jnp.float32),
            dma((parts, columns, 2)),
            dma((parts, columns, 2)),
            dma((parts, columns, 2)),
            dma((parts, columns)),
            dma((kinds, 2, groups + halves)),
            dma((kinds, 2, groups * halves)),
            dma((kinds, 2, groups, halves)),
            dma((kinds, members, 2)),
            dma((1 + parts, members)),
            dma((1 + parts, members)),
            dma((columns, 2)),
            dma((columns,)),
            dma((2, max(members, columns))),
            dma((2, max(members, columns))),
            dma((3,)),
        ],
        compiler_params=pltpu.CompilerParams(
            collective_id=1, has_side_effects=True, vmem_limit_bytes=62 * 1024 * 1024
        ),
        cost_estimate=pl.CostEstimate(
            flops=2 * full * full * full // 4, bytes_accessed=full * width * 8, transcendentals=0
        ),
    )(acts, panel, rotation)


def shards(embeddings, layer_weight, rotation):
    full = layer_weight.shape[1]
    head = (rotation / math.sqrt(full)).astype(HALF)
    panel = lax.all_gather(head, ROWS, axis=0, tiled=True)
    acts = run_layers(embeddings, layer_weight)
    return run_update(acts, panel, rotation, embeddings.shape[0] * lax.axis_size("dp"))


def solution(mesh):
    return jax.shard_map(
        shards,
        mesh=mesh,
        in_specs=(P("dp", "tensor"), P("layer", None, "tensor"), P(("dp", "layer"), "tensor")),
        out_specs=P(("dp", "layer"), "tensor"),
        check_vma=False,
    )
```
